256 devices in a mesh: pipe: 2 (over y_lo), patch: 16 (over x, y_hi, core), hour: 8 (over z).
Axes of the slice: x: 4, y: 4 (y_hi: 2, y_lo: 2; y = y_hi * 2 + y_lo), z: 8, core: 2. Of those that a mesh axis runs over, the one named last changes fastest.
Arguments:
- inputs: bfloat16 [2, 256, 128, 512], P(None, 'patch', 'hour'), may hold values from -6 to 6
- visibility: int32 [4, 2], replicated, may hold values from 0 to 3, all different within a row
- norm_gains: float32 [2, 3, 512], P('pipe'), may hold values from 0.1 to 1.9
- scales: float32 [2, 2, 8], P('pipe'), may hold values from 2 to 12
- mixer_in: bfloat16 [2, 2, 512, 1536], P('pipe'), may hold values from -0.25 to 0.25
- mixer_out: bfloat16 [2, 2, 512, 512], P('pipe'), may hold values from -0.25 to 0.25
- expand_weight: bfloat16 [2, 512, 2048], P('pipe'), may hold values from -0.25 to 0.25
- reduce_weight: bfloat16 [2, 2048, 512], P('pipe'), may hold values from -0.125 to 0.125
Outputs:
- outputs: bfloat16 [2, 256, 128, 512], P(None, 'patch', 'hour')
The draws below stay inside these ranges and needn't reach their ends.
Inputs may be any that keep to these rules, and one draw needn't show every extreme that they name: `visibility`: row b lists 2 different key blocks of 64 patches for query block b; every block is listed in some row.
All inputs are finite; a program needn't handle non-finite values.
Results may differ from the reference program's by a relative error of at most 0.023.
Values may be sent and summed in bfloat16 or wider, within the bound.
A program may use at most 64 MiB of HBM per device.

```python
import math
import jax
import jax.numpy as jnp
from jax import lax

D = 512
HEADS = 8
HEAD_DIM = 64
FF = 2048
PB = 64
KV = 2
MICRO = 2
P_SIZE = 256
H = 128
NB = 4


def block_scale(key, dims, cuts, low, high):
    loudness = 1.0
    for position, blocks in cuts:
        steps = jax.random.uniform(jax.random.fold_in(jax.random.fold_in(key, 6), position), (blocks,), jnp.float32, low / len(cuts), high / len(cuts))
        loudness = loudness * jnp.repeat(jnp.exp(steps), dims[position] // blocks).reshape((-1,) + (1,) * (len(dims) - 1 - position))
    return loudness


def different_ones(key, rows, number_of, top, lift):
    sequence = jax.random.permutation(jax.random.fold_in(key, 1), number_of)
    boost = sequence
    for power in range(3):
        boost = boost * boost // number_of
    boost = boost * lift // number_of
    tickets = jax.random.randint(jax.random.fold_in(key, 2), (rows, number_of), 0, 4096) + boost
    sure = jax.random.permutation(jax.random.fold_in(key, 3), rows)[jnp.arange(number_of) % rows]
    tickets = jnp.where(jnp.arange(rows)[:, None] == sure[None, :], 1 << 14, tickets)
    priority = tickets * number_of + jnp.arange(number_of)
    return lax.top_k(priority.astype(jnp.int32), top)[1].astype(jnp.int32)


def bell_draw(stream_key, extent, deviation, limit, split=(), held_as=jnp.bfloat16):
    entries = jax.random.normal(stream_key, extent, jnp.float32) * deviation
    if len(split) > 0:
        entries = block_scale(stream_key, extent, split, -0.22, 0.18) * entries
    return jnp.clip(entries, min=-limit, max=limit).astype(held_as)


def setup_inputs(seed: int = 0) -> dict:
    key_list = jax.random.split(jax.random.key(seed), 9)
    inputs = bell_draw(key_list[0], (MICRO, P_SIZE, H, D), 1.0, 6.0, ((1, 16), (2, 8)))
    visibility = different_ones(key_list[1], NB, NB, KV, 4096)
    norm_gains = jnp.clip(1.0 + 0.18 * jax.random.normal(key_list[2], (2, 3, D), jnp.float32), 0.1, 1.9)
    scales = jnp.clip(jnp.exp(math.log(12.0) - 1.7917595 * jax.random.uniform(key_list[3], (2, 2, HEADS), jnp.float32) ** block_scale(key_list[3], (2, 2, HEADS), ((0, 2),), -0.2, 0.2)), 2.0, 12.0)
    mixer_in = bell_draw(key_list[4], (2, 2, D, 3 * D), D ** -0.5, 0.25, ((0, 2),))
    mixer_out = bell_draw(key_list[5], (2, 2, D, D), D ** -0.5, 0.25, ((0, 2),))
    expand_weight = bell_draw(key_list[6], (2, D, FF), D ** -0.5, 0.25, ((0, 2),))
    reduce_weight = bell_draw(key_list[7], (2, FF, D), FF ** -0.5, 0.125, ((0, 2),))
    return dict(inputs=inputs, visibility=visibility, norm_gains=norm_gains, scales=scales, mixer_in=mixer_in, mixer_out=mixer_out, expand_weight=expand_weight, reduce_weight=reduce_weight)


def rms_norm(values, gain):
    values = values.astype(jnp.float32)
    factor = lax.rsqrt(lax.optimization_barrier(jnp.mean(values * values, axis=-1, keepdims=True)) + 1e-05)
    return (values * factor * gain).astype(jnp.bfloat16)

def head_norm(values):
    factor = lax.rsqrt(lax.optimization_barrier(jnp.mean(values * values, axis=-1, keepdims=True)) + 1e-06)
    return (values * factor).astype(jnp.bfloat16)

def split_heads(projected, lead_shape):
    width = projected.shape[-1] // 3
    shape = lead_shape + (HEADS, HEAD_DIM)
    queries = head_norm(projected[:, :width].reshape(shape))
    keys_all = head_norm(projected[:, width:2 * width].reshape(shape))
    values = projected[:, 2 * width:].astype(jnp.bfloat16).reshape(shape)
    return (queries, keys_all, values)

def softmax_weights(scores, scale):
    scaled = scores * (scale / HEAD_DIM)[:, None, None]
    powers = jnp.exp(scaled)
    return (powers / lax.optimization_barrier(jnp.sum(powers, axis=-1, keepdims=True))).astype(jnp.bfloat16)

def time_group(group, scale):
    queries, keys_all, values = group
    scores = jnp.einsum('pqnd,pknd->pnqk', queries.astype(jnp.float32), keys_all.astype(jnp.float32))
    weights = softmax_weights(scores, scale)
    mixed = jnp.einsum('pnqk,pknd->pqnd', weights.astype(jnp.float32), values.astype(jnp.float32))
    return mixed.astype(jnp.bfloat16)

def time_mix(tokens, gain, weight_in, weight_out, scale):
    count_p, count_h, width = tokens.shape
    normed = rms_norm(tokens, gain).reshape(-1, width)
    projected = jnp.dot(normed, weight_in, preferred_element_type=jnp.float32)
    parts = split_heads(projected, (count_p, count_h))
    grouped = tuple((item.reshape(count_p // 8, 8, count_h, HEADS, HEAD_DIM) for item in parts))
    attended = lax.map(lambda group: time_group(group, scale), grouped).reshape(-1, width)
    update = jnp.dot(attended, weight_out, preferred_element_type=jnp.float32)
    return (tokens.astype(jnp.float32) + update.reshape(tokens.shape)).astype(jnp.bfloat16)

def patch_hour(group, visibility, scale):
    queries, keys_all, values = group
    count = queries.shape[0]
    blocks = count // PB
    query_blocks = queries.reshape(blocks, PB, HEADS, HEAD_DIM)
    key_blocks = jnp.take(keys_all.reshape(blocks, PB, HEADS, HEAD_DIM), visibility, axis=0).reshape(blocks, KV * PB, HEADS, HEAD_DIM)
    value_blocks = jnp.take(values.reshape(blocks, PB, HEADS, HEAD_DIM), visibility, axis=0).reshape(blocks, KV * PB, HEADS, HEAD_DIM)
    scores = jnp.einsum('bqnd,bknd->bnqk', query_blocks.astype(jnp.float32), key_blocks.astype(jnp.float32))
    weights = softmax_weights(scores, scale)
    mixed = jnp.einsum('bnqk,bknd->bqnd', weights.astype(jnp.float32), value_blocks.astype(jnp.float32))
    return mixed.astype(jnp.bfloat16).reshape(count, HEADS, HEAD_DIM)

def patch_mix(tokens, visibility, gain, weight_in, weight_out, scale):
    count_p, count_h, width = tokens.shape
    normed = rms_norm(tokens, gain).reshape(-1, width)
    projected = jnp.dot(normed, weight_in, preferred_element_type=jnp.float32)
    parts = split_heads(projected, (count_p, count_h))
    moved = tuple((jnp.moveaxis(item, 1, 0) for item in parts))
    attended = lax.map(lambda group: patch_hour(group, visibility, scale), moved)
    attended = jnp.moveaxis(attended, 0, 1).reshape(-1, width)
    update = jnp.dot(attended, weight_out, preferred_element_type=jnp.float32)
    return (tokens.astype(jnp.float32) + update.reshape(tokens.shape)).astype(jnp.bfloat16)

def feed_forward(tokens, gain, weight_up, weight_down):
    width = tokens.shape[-1]
    normed = rms_norm(tokens, gain).reshape(-1, width)
    hidden = jax.nn.gelu(jnp.dot(normed, weight_up, preferred_element_type=jnp.float32)).astype(jnp.bfloat16)
    update = jnp.dot(hidden, weight_down, preferred_element_type=jnp.float32)
    return (tokens.astype(jnp.float32) + update.reshape(tokens.shape)).astype(jnp.bfloat16)

def run_block(tokens, visibility, gains, scales, mixer_in, mixer_out, expand_weight, reduce_weight):
    tokens = time_mix(tokens, gains[0], mixer_in[0], mixer_out[0], scales[0])
    tokens = patch_mix(tokens, visibility, gains[1], mixer_in[1], mixer_out[1], scales[1])
    return feed_forward(tokens, gains[2], expand_weight, reduce_weight)

def reference(inputs, visibility, norm_gains, scales, mixer_in, mixer_out, expand_weight, reduce_weight):
    finished = []
    for number in range(MICRO):
        tokens = inputs[number]
        for section in range(2):
            tokens = run_block(tokens, visibility, norm_gains[section], scales[section], mixer_in[section], mixer_out[section], expand_weight[section], reduce_weight[section])
        finished.append(tokens)
    return jnp.stack(finished)
```

```python
import functools
import math

import jax
import jax.numpy as jnp
from jax import lax
from jax.experimental import pallas as pl
from jax.experimental.pallas import tpu as pltpu
from jax.sharding import PartitionSpec as P

HEADS = 8
HEAD_DIM = 64
PB = 64
KV = 2
BF = jnp.bfloat16
F32 = jnp.float32
MESH = pl.DeviceIdType.MESH


def iota(shape, axis):
    return lax.broadcasted_iota(jnp.int32, shape, axis)


def dot(a, b):
    return jnp.dot(a, b, preferred_element_type=F32)


def dot_nt(a, b):
    return lax.dot_general(a, b, (((1,), (1,)), ((), ())), preferred_element_type=F32)


def rms(x, gain):
    x = x.astype(F32)
    factor = lax.rsqrt(jnp.mean(x * x, axis=-1, keepdims=True) + 1e-05)
    return (x * factor * gain).astype(BF)


def fill_constants(turn, same_head, pair_sums):
    r, c = iota((256, 256), 0), iota((256, 256), 1)
    turn[...] = jnp.where(c == (r % 16) * 16 + r // 16, 1.0, 0.0).astype(BF)
    same_head[...] = jnp.where(r // HEAD_DIM == c // HEAD_DIM, 1.0, 0.0).astype(BF)
    r, c = iota((256, 128), 0), iota((256, 128), 1)
    pair_sums[...] = jnp.where(r // 128 == c // HEAD_DIM, 1.0, 0.0).astype(BF)


def project(normed, which, weight_in, scales, same_head, q_s, ke_s, ko_s, ve_s, vo_s):
    width = 2 * 256
    lane = iota((1, 256), 1)
    even = (lane // HEAD_DIM) % 2 == 0
    zero = jnp.zeros((256, 256), BF)
    for part in range(3):
        for half in range(2):
            at = pl.ds(half * 256, 256)
            value = dot(normed, weight_in[which, :, pl.ds(part * width + half * 256, 256)])
            if part < 2:
                squares = dot((value * value).astype(BF), same_head[...])
                value = value * lax.rsqrt(squares * (1.0 / HEAD_DIM) + 1e-06)
            if part == 0:
                row = jnp.zeros((1, 256), F32)
                for n in range(4):
                    scale = scales[0, which, half * 4 + n] * (math.log2(math.e) / HEAD_DIM)
                    row = jnp.where(lane // HEAD_DIM == n, scale, row)
                q_s[:, at] = (value * row).astype(BF)
            else:
                even_s, odd_s = (ke_s, ko_s) if part == 1 else (ve_s, vo_s)
                value = value.astype(BF)
                even_s[:, :, at] = jnp.where(even, value, zero).reshape(4, PB, 256)
                odd_s[:, :, at] = jnp.where(even, zero, value).reshape(4, PB, 256)


def attend(queries, keys, values, pair_sums):
    weights = jnp.exp2(dot_nt(queries, keys)).astype(BF)
    mixed = dot(weights, jnp.concatenate([values, pair_sums], axis=1))
    return (mixed[:, :128] / mixed[:, 128:]).astype(BF)


def gelu(u):
    return 0.5 * u * (1.0 + jnp.tanh(math.sqrt(2.0 / math.pi) * (u + 0.044715 * (u * u * u))))


def time_stage(x, gains, scales, w_in, w_out, same_head, pair_sums, q_s, ke_s, ko_s, ve_s, vo_s, att_s):
    normed = rms(x, gains[0, 0:1, :])
    project(normed, 0, w_in, scales, same_head, q_s, ke_s, ko_s, ve_s, vo_s)
    for a in range(2):
        rows = pl.ds(a * 128, 128)
        for j in range(4):
            at = pl.ds(j * 128, 128)
            keys = jnp.concatenate([k[2 * a + i, :, at] for k in (ke_s, ko_s) for i in range(2)], axis=0)
            values = jnp.concatenate([v[2 * a + i, :, at] for v in (ve_s, vo_s) for i in range(2)], axis=0)
            att_s[rows, at] = attend(q_s[rows, at], keys, values, pair_sums[...])
    return (x.astype(F32) + dot(att_s[...], w_out[0])).astype(BF)


def patch_stage(
    x, vis, gains, scales, w_in, w_out, same_head, pair_sums, q_s, ke_s, ko_s, ve_s, vo_s, att_s
):
    normed = rms(x, gains[0, 1:2, :])
    project(normed, 1, w_in, scales, same_head, q_s, ke_s, ko_s, ve_s, vo_s)
    for b in range(4):
        rows = pl.ds(b * PB, PB)
        seen = [vis[b, i] for i in range(KV)]
        for j in range(4):
            at = pl.ds(j * 128, 128)
            keys = jnp.concatenate([s[z, :, at] for s in (ke_s, ko_s) for z in seen], axis=0)
            values = jnp.concatenate([s[z, :, at] for s in (ve_s, vo_s) for z in seen], axis=0)
            att_s[rows, at] = attend(q_s[rows, at], keys, values, pair_sums[...])
    return (x.astype(F32) + dot(att_s[...], w_out[1])).astype(BF)


def feed_forward(x, gains, up, down, hidden):
    normed = rms(x, gains[0, 2:3, :])
    for c in range(8):
        at = pl.ds(c * 256, 256)
        hidden[:, at] = gelu(dot(normed, up[:, at])).astype(BF)
    return (x.astype(F32) + dot(hidden[...], down[...])).astype(BF)


def loop(start, stop, body):
    def step(i, carry):
        body(i)
        return carry

    lax.fori_loop(start, stop, step, 0)


def kernel(
    n_patch,
    n_hour,
    vis,
    scales,
    gains,
    inputs,
    w_in_hbm,
    w_out_hbm,
    up_hbm,
    down_hbm,
    out,
    w_in,
    w_out,
    up,
    down,
    timed,
    mixed,
    homed,
    turned,
    spread,
    result,
    back,
    handed,
    final,
    turn,
    same_head,
    pair_sums,
    q_s,
    ke_s,
    ko_s,
    ve_s,
    vo_s,
    att_s,
    hidden,
    w_sem,
    timed_sem,
    homed_sem,
    spread_sem,
    back_sem,
    out_sem,
    in_send,
    mixed_send,
    turned_send,
    result_send,
    final_send,
    handed_send,
):
    s = lax.axis_index("pipe")
    p = lax.axis_index("patch")
    h = lax.axis_index("hour")

    loads = [
        pltpu.make_async_copy(src.at[0], dst, w_sem.at[i])
        for i, (src, dst) in enumerate(
            [(w_in_hbm, w_in), (w_out_hbm, w_out), (up_hbm, up), (down_hbm, down)]
        )
    ]
    for load in loads:
        load.start()

    def at16(i):
        return pl.ds(pl.multiple_of(i * 16, 16), 16)

    def remote(src, dst, send, recv, device):
        pltpu.make_async_remote_copy(
            src_ref=src,
            dst_ref=dst,
            send_sem=send,
            recv_sem=recv,
            device_id=device,
            device_id_type=MESH,
        ).start()

    def arrive(ref, sem):
        pltpu.make_async_copy(ref, ref, sem).wait()

    barrier = pltpu.get_barrier_semaphore()

    def greet(device):
        pl.semaphore_signal(barrier, inc=1, device_id=device, device_id_type=MESH)

    loop(1, n_hour, lambda k: greet((s, p, lax.rem(h + k, n_hour))))
    loop(1, n_patch, lambda k: greet((s, lax.rem(p + k, n_patch), h)))

    @pl.when(s == 0)
    def _():
        loop(0, n_patch, lambda k: greet((1, k, h)))

    @pl.when(s == 1)
    def _():
        loop(0, n_hour, lambda k: greet((0, p, k)))

    fill_constants(turn, same_head, pair_sums)

    @pl.when(s == 0)
    def _():
        pl.semaphore_wait(barrier, (n_hour - 1) + (n_patch - 1) + n_hour)

    @pl.when(s == 1)
    def _():
        pl.semaphore_wait(barrier, (n_hour - 1) + (n_patch - 1) + n_patch)

    def send_inputs(m):
        def one(k):
            d = lax.rem(h + k, n_hour)
            remote(
                inputs.at[m, pl.ds(2 * d, 2)],
                timed.at[m, :, at16(h)],
                in_send.at[m, k],
                timed_sem.at[m, h],
                (0, p, d),
            )

        loop(1, n_hour, one)
        pltpu.make_async_copy(
            inputs.at[m, pl.ds(2 * h, 2)], timed.at[m, :, at16(h)], timed_sem.at[m, h]
        ).start()

    @pl.when(s == 0)
    def _():
        send_inputs(0)

    loads[0].wait()
    loads[1].wait()

    def time_step(m):
        loop(0, n_hour, lambda k: arrive(timed.at[m, :, at16(k)], timed_sem.at[m, k]))

        @pl.when((s == 0) & (m == 0))
        def _():
            send_inputs(1)

        x = timed[m].reshape(256, 512)
        y = time_stage(
            x, gains, scales, w_in, w_out, same_head, pair_sums, q_s, ke_s, ko_s, ve_s, vo_s, att_s
        )
        mixed[m] = y.reshape(2, 128, 512)

        def one(k):
            d = lax.rem(h + k, n_hour)
            remote(
                mixed.at[m, :, at16(d)],
                homed.at[m, pl.ds(2 * h, 2)],
                mixed_send.at[m, k],
                homed_sem.at[m, h],
                (s, p, d),
            )

        loop(1, n_hour, one)
        pltpu.make_async_copy(
            mixed.at[m, :, at16(h)], homed.at[m, pl.ds(2 * h, 2)], homed_sem.at[m, h]
        ).start()

    loop(0, 2, time_step)

    def spread_step(m):
        loop(0, n_hour, lambda k: arrive(homed.at[m, pl.ds(2 * k, 2)], homed_sem.at[m, k]))
        turned[m] = dot(turn[...], homed[m].reshape(256, 512)).astype(BF).reshape(16, 16, 512)

        def one(k):
            d = lax.rem(p + k, n_patch)
            remote(
                turned.at[m, d],
                spread.at[m, at16(p)],
                turned_send.at[m, k],
                spread_sem.at[m, p],
                (s, d, h),
            )

        loop(1, n_patch, one)
        pltpu.make_async_copy(turned.at[m, p], spread.at[m, at16(p)], spread_sem.at[m, p]).start()

    loop(0, 2, spread_step)
    loads[2].wait()
    loads[3].wait()

    def patch_step(m):
        loop(0, n_patch, lambda k: arrive(spread.at[m, at16(k)], spread_sem.at[m, k]))
        y = patch_stage(
            spread[m],
            vis,
            gains,
            scales,
            w_in,
            w_out,
            same_head,
            pair_sums,
            q_s,
            ke_s,
            ko_s,
            ve_s,
            vo_s,
            att_s,
        )
        result[m] = feed_forward(y, gains, up, down, hidden)

        def one(k):
            d = lax.rem(p + k, n_patch)
            remote(
                result.at[m, at16(d)],
                back.at[s, m, p],
                result_send.at[m, k],
                back_sem.at[s, m, p],
                (s, d, h),
            )

        loop(1, n_patch, one)
        pltpu.make_async_copy(result.at[m, at16(p)], back.at[s, m, p], back_sem.at[s, m, p]).start()

        @pl.when(s == 1)
        def _():
            def other(k):
                d = lax.rem(p + k, n_patch)
                remote(
                    result.at[m, at16(d)],
                    back.at[1, m, p],
                    final_send.at[m, k],
                    back_sem.at[1, m, p],
                    (0, d, h),
                )

            loop(0, n_patch, other)

    loop(0, 2, patch_step)

    def turn_back(b, m):
        loop(0, n_patch, lambda k: arrive(back.at[b, m, k], back_sem.at[b, m, k]))
        return dot(turn[...], back[b, m].reshape(256, 512)).astype(BF).reshape(16, 16, 512)

    @pl.when(s == 0)
    def _():
        def hand_step(m):
            handed[m] = turn_back(0, m)

            def one(k):
                d = lax.rem(h + k, n_hour)
                remote(
                    handed.at[m, pl.ds(2 * d, 2)],
                    timed.at[m, :, at16(h)],
                    handed_send.at[m, k],
                    timed_sem.at[m, h],
                    (1, p, d),
                )

            loop(0, n_hour, one)

        loop(0, 2, hand_step)

    def final_step(m):
        final[m] = turn_back(1, m)
        pltpu.make_async_copy(final.at[m], out.at[m], out_sem.at[m]).start()

    loop(0, 2, final_step)

    def finish(m):
        def hours(k):
            arrive(mixed.at[m, :, at16(k)], mixed_send.at[m, k])

        def patches(k):
            arrive(turned.at[m, k], turned_send.at[m, k])
            arrive(result.at[m, at16(k)], result_send.at[m, k])

        loop(1, n_hour, hours)
        loop(1, n_patch, patches)

        @pl.when(s == 0)
        def _():
            loop(1, n_hour, lambda k: arrive(timed.at[m, :, at16(k)], in_send.at[m, k]))
            loop(0, n_hour, lambda k: arrive(handed.at[m, pl.ds(2 * k, 2)], handed_send.at[m, k]))

        @pl.when(s == 1)
        def _():
            loop(0, n_patch, lambda k: arrive(result.at[m, at16(k)], final_send.at[m, k]))

        pltpu.make_async_copy(final.at[m], out.at[m], out_sem.at[m]).wait()

    loop(0, 2, finish)


def solution(mesh):
    n_patch, n_hour = mesh.shape["patch"], mesh.shape["hour"]
    placed = (
        P(None, "patch", "hour", None),
        P(),
        P("pipe", None, None),
        P("pipe", None, None),
        P("pipe", None, None, None),
        P("pipe", None, None, None),
        P("pipe", None, None),
        P("pipe", None, None),
    )

    def local(inputs, visibility, norm_gains, scales, mixer_in, mixer_out, expand, reduce):
        tile = (256, 512)
        scratch = [
            pltpu.VMEM((2, 512, 1536), BF),
            pltpu.VMEM((2, 512, 512), BF),
            pltpu.VMEM((512, 2048), BF),
            pltpu.VMEM((2048, 512), BF),
            pltpu.VMEM((2, 2, 128, 512), BF),
            pltpu.VMEM((2, 2, 128, 512), BF),
            pltpu.VMEM((2, 16, 16, 512), BF),
            pltpu.VMEM((2, 16, 16, 512), BF),
            pltpu.VMEM((2, 256, 512), BF),
            pltpu.VMEM((2, 256, 512), BF),
            pltpu.VMEM((2, 2, 16, 16, 512), BF),
            pltpu.VMEM((2, 16, 16, 512), BF),
            pltpu.VMEM((2, 16, 16, 512), BF),
            pltpu.VMEM((256, 256), BF),
            pltpu.VMEM((256, 256), BF),
            pltpu.VMEM((256, 128), BF),
        ]
        scratch += [pltpu.VMEM(tile, BF)]
        scratch += [pltpu.VMEM((4, PB, 512), BF)] * 4
        scratch += [pltpu.VMEM(tile, BF)]
        scratch += [pltpu.VMEM((256, 2048), BF)]
        dma = pltpu.SemaphoreType.DMA
        scratch += [
            dma((4,)),
            dma((2, n_hour)),
            dma((2, n_hour)),
            dma((2, n_patch)),
            dma((2, 2, n_patch)),
            dma((2,)),
            dma((2, n_hour)),
            dma((2, n_hour)),
            dma((2, n_patch)),
            dma((2, n_patch)),
            dma((2, n_patch)),
            dma((2, n_hour)),
        ]
        smem = pl.BlockSpec(memory_space=pltpu.SMEM)
        hbm = pl.BlockSpec(memory_space=pl.ANY)
        return pl.pallas_call(
            functools.partial(kernel, n_patch, n_hour),
            out_shape=jax.ShapeDtypeStruct(inputs.shape, inputs.dtype),
            in_specs=[smem, smem, pl.BlockSpec(memory_space=pltpu.VMEM)] + [hbm] * 5,
            out_specs=hbm,
            scratch_shapes=scratch,
            compiler_params=pltpu.CompilerParams(collective_id=0, has_side_effects=True),
            name="space_time_blocks",
        )(visibility, scales, norm_gains, inputs, mixer_in, mixer_out, expand, reduce)

    return jax.shard_map(
        local, mesh=mesh, in_specs=placed, out_specs=P(None, "patch", "hour", None), check_vma=False
    )
```

```python
import functools
import math

import jax
import jax.numpy as jnp
from jax import lax
from jax.experimental import pallas as pl
from jax.experimental.pallas import tpu as pltpu
from jax.sharding import PartitionSpec as P

HEADS = 8
HEAD_DIM = 64
PB = 64
KV = 2
BF = jnp.bfloat16
F32 = jnp.float32
MESH = pl.DeviceIdType.MESH


def iota(shape, axis):
    return lax.broadcasted_iota(jnp.int32, shape, axis)


def dot(a, b):
    return jnp.dot(a, b, preferred_element_type=F32)


def dot_nt(a, b):
    return lax.dot_general(a, b, (((1,), (1,)), ((), ())), preferred_element_type=F32)


def rms(x, gain):
    x = x.astype(F32)
    factor = lax.rsqrt(jnp.mean(x * x, axis=-1, keepdims=True) + 1e-05)
    return (x * factor * gain).astype(BF)


def fill_constants(turn, same_head, pair_sums):
    r, c = iota((256, 256), 0), iota((256, 256), 1)
    turn[...] = jnp.where(c == (r % 16) * 16 + r // 16, 1.0, 0.0).astype(BF)
    same_head[...] = jnp.where(r // HEAD_DIM == c // HEAD_DIM, 1.0, 0.0).astype(BF)
    r, c = iota((256, 128), 0), iota((256, 128), 1)
    pair_sums[...] = jnp.where(r // 128 == c // HEAD_DIM, 1.0, 0.0).astype(BF)


def project(normed, which, weight_in, scales, same_head, q_s, ke_s, ko_s, ve_s, vo_s):
    width = 2 * 256
    lane = iota((1, 256), 1)
    even = (lane // HEAD_DIM) % 2 == 0
    zero = jnp.zeros((256, 256), BF)
    for part in range(3):
        for half in range(2):
            at = pl.ds(half * 256, 256)
            value = dot(normed, weight_in[which, :, pl.ds(part * width + half * 256, 256)])
            if part < 2:
                squares = dot((value * value).astype(BF), same_head[...])
                value = value * lax.rsqrt(squares * (1.0 / HEAD_DIM) + 1e-06)
            if part == 0:
                row = jnp.zeros((1, 256), F32)
                for n in range(4):
                    scale = scales[0, which, half * 4 + n] * (math.log2(math.e) / HEAD_DIM)
                    row = jnp.where(lane // HEAD_DIM == n, scale, row)
                q_s[:, at] = (value * row).astype(BF)
            else:
                even_s, odd_s = (ke_s, ko_s) if part == 1 else (ve_s, vo_s)
                value = value.astype(BF)
                even_s[:, :, at] = jnp.where(even, value, zero).reshape(4, PB, 256)
                odd_s[:, :, at] = jnp.where(even, zero, value).reshape(4, PB, 256)


def attend(queries, keys, values, pair_sums):
    weights = jnp.exp2(dot_nt(queries, keys)).astype(BF)
    mixed = dot(weights, jnp.concatenate([values, pair_sums], axis=1))
    return (mixed[:, :128] / mixed[:, 128:]).astype(BF)


def gelu(u):
    return 0.5 * u * (1.0 + jnp.tanh(math.sqrt(2.0 / math.pi) * (u + 0.044715 * (u * u * u))))


def time_stage(x, gains, scales, w_in, w_out, same_head, pair_sums, q_s, ke_s, ko_s, ve_s, vo_s, att_s):
    normed = rms(x, gains[0])
    project(normed, 0, w_in, scales, same_head, q_s, ke_s, ko_s, ve_s, vo_s)
    for a in range(2):
        rows = pl.ds(a * 128, 128)
        for j in range(4):
            at = pl.ds(j * 128, 128)
            keys = jnp.concatenate([k[2 * a + i, :, at] for k in (ke_s, ko_s) for i in range(2)], axis=0)
            values = jnp.concatenate([v[2 * a + i, :, at] for v in (ve_s, vo_s) for i in range(2)], axis=0)
            att_s[rows, at] = attend(q_s[rows, at], keys, values, pair_sums[...])
    return (x.astype(F32) + dot(att_s[...], w_out[0])).astype(BF)


def patch_stage(
    x, vis, gains, scales, w_in, w_out, same_head, pair_sums, q_s, ke_s, ko_s, ve_s, vo_s, att_s
):
    normed = rms(x, gains[1])
    project(normed, 1, w_in, scales, same_head, q_s, ke_s, ko_s, ve_s, vo_s)
    for b in range(4):
        rows = pl.ds(b * PB, PB)
        seen = [vis[i, b] for i in range(KV)]
        for j in range(4):
            at = pl.ds(j * 128, 128)
            keys = jnp.concatenate([s[z, :, at] for s in (ke_s, ko_s) for z in seen], axis=0)
            values = jnp.concatenate([s[z, :, at] for s in (ve_s, vo_s) for z in seen], axis=0)
            att_s[rows, at] = attend(q_s[rows, at], keys, values, pair_sums[...])
    return (x.astype(F32) + dot(att_s[...], w_out[1])).astype(BF)


def feed_forward(x, gains, up, down, hidden):
    normed = rms(x, gains[2])
    for c in range(8):
        at = pl.ds(c * 256, 256)
        hidden[:, at] = gelu(dot(normed, up[:, at])).astype(BF)
    return (x.astype(F32) + dot(hidden[...], down[...])).astype(BF)


def hour_order(h, n_hour, with_self):
    half = n_hour // 2
    steps = [half] + [k for i in range(half - 1, 0, -1) for k in (i, n_hour - i)] + [0] * with_self
    return [(k, lax.rem(h + k, n_hour)) for k in steps]


def patch_order(p, n_patch, with_self):
    x, y, c = p // 4, lax.rem(p // 2, 2), lax.rem(p, 2)
    steps = [(dx, dy, dc) for dy in (1, 0) for dx in (2, 1, 3, 0) for dc in (0, 1)]
    steps.sort(key=lambda t: (-(min(t[0], 4 - t[0]) + 2 * t[1]), -t[2]))
    order = []
    for k, (dx, dy, dc) in enumerate(steps):
        if (dx, dy, dc) != (0, 0, 0) or with_self:
            d = lax.rem(x + dx, n_patch // 4) * 4 + lax.rem(y + dy, 2) * 2 + lax.rem(c + dc, 2)
            order.append((k, d))
    return order


def loop(start, stop, body):
    def step(i, carry):
        body(i)
        return carry

    lax.fori_loop(start, stop, step, 0)


def kernel(
    n_patch,
    n_hour,
    vis,
    scales,
    gains,
    inputs,
    w_in_hbm,
    w_out_hbm,
    up_hbm,
    down_hbm,
    out,
    w_in,
    w_out,
    up,
    down,
    timed,
    mixed,
    homed,
    turned,
    spread,
    result,
    back,
    handed,
    final,
    turn,
    same_head,
    pair_sums,
    q_s,
    ke_s,
    ko_s,
    ve_s,
    vo_s,
    att_s,
    hidden,
    w_sem,
    timed_sem,
    homed_sem,
    spread_sem,
    back_sem,
    out_sem,
    in_send,
    mixed_send,
    turned_send,
    result_send,
    final_send,
    handed_send,
):
    s = lax.axis_index("pipe")
    p = lax.axis_index("patch")
    h = lax.axis_index("hour")

    loads = [
        pltpu.make_async_copy(src.at[0], dst, w_sem.at[i])
        for i, (src, dst) in enumerate(
            [(w_in_hbm, w_in), (w_out_hbm, w_out), (up_hbm, up), (down_hbm, down)]
        )
    ]
    for load in loads:
        load.start()

    def at16(i):
        return pl.ds(pl.multiple_of(i * 16, 16), 16)

    def remote(src, dst, send, recv, device):
        pltpu.make_async_remote_copy(
            src_ref=src,
            dst_ref=dst,
            send_sem=send,
            recv_sem=recv,
            device_id=device,
            device_id_type=MESH,
        ).start()

    def arrive(ref, sem):
        pltpu.make_async_copy(ref, ref, sem).wait()

    barrier = pltpu.get_barrier_semaphore()

    def greet(device):
        pl.semaphore_signal(barrier, inc=1, device_id=device, device_id_type=MESH)

    loop(1, n_hour, lambda k: greet((s, p, lax.rem(h + k, n_hour))))
    loop(1, n_patch, lambda k: greet((s, lax.rem(p + k, n_patch), h)))
    loop(0, n_hour, lambda k: greet((1 - s, p, k)))

    @pl.when(s == 0)
    def _():
        loop(0, n_patch, lambda k: greet((1, k, h)))

    fill_constants(turn, same_head, pair_sums)

    @pl.when(s == 0)
    def _():
        pl.semaphore_wait(barrier, (n_hour - 1) + (n_patch - 1) + n_hour)

    @pl.when(s == 1)
    def _():
        pl.semaphore_wait(barrier, (n_hour - 1) + (n_patch - 1) + n_hour + n_patch)

    def send_input(m, k, d):
        remote(
            inputs.at[m, pl.ds(2 * d, 2)],
            timed.at[m, :, at16(h)],
            in_send.at[k],
            timed_sem.at[m, h],
            (0, p, d),
        )

    @pl.when(s == 0)
    def _():
        for k, d in hour_order(h, n_hour, False):
            send_input(0, k, d)
        pltpu.make_async_copy(
            inputs.at[0, pl.ds(2 * h, 2)], timed.at[0, :, at16(h)], timed_sem.at[0, h]
        ).start()

    @pl.when(s == 1)
    def _():
        for k, d in hour_order(h, n_hour, True):
            send_input(1, k, d)

    loads[0].wait()
    loads[1].wait()

    def time_step(m):
        loop(0, n_hour, lambda k: arrive(timed.at[m, :, at16(k)], timed_sem.at[m, k]))

        x = timed[m].reshape(256, 512)
        y = time_stage(
            x, gains, scales, w_in, w_out, same_head, pair_sums, q_s, ke_s, ko_s, ve_s, vo_s, att_s
        )
        mixed[m] = y.reshape(2, 128, 512)

        for k, d in hour_order(h, n_hour, False):
            remote(
                mixed.at[m, :, at16(d)],
                homed.at[m, pl.ds(2 * h, 2)],
                mixed_send.at[m, k],
                homed_sem.at[m, h],
                (s, p, d),
            )
        pltpu.make_async_copy(
            mixed.at[m, :, at16(h)], homed.at[m, pl.ds(2 * h, 2)], homed_sem.at[m, h]
        ).start()

    loop(0, 2, time_step)

    def spread_step(m):
        loop(0, n_hour, lambda k: arrive(homed.at[m, pl.ds(2 * k, 2)], homed_sem.at[m, k]))
        turned[m] = dot(turn[...], homed[m].reshape(256, 512)).astype(BF).reshape(16, 16, 512)

        for k, d in patch_order(p, n_patch, False):
            remote(
                turned.at[m, d],
                spread.at[m, at16(p)],
                turned_send.at[m, k],
                spread_sem.at[m, p],
                (s, d, h),
            )
        pltpu.make_async_copy(turned.at[m, p], spread.at[m, at16(p)], spread_sem.at[m, p]).start()

    loop(0, 2, spread_step)
    loads[2].wait()
    loads[3].wait()

    def patch_step(m):
        loop(0, n_patch, lambda k: arrive(spread.at[m, at16(k)], spread_sem.at[m, k]))
        y = patch_stage(
            spread[m],
            vis,
            gains,
            scales,
            w_in,
            w_out,
            same_head,
            pair_sums,
            q_s,
            ke_s,
            ko_s,
            ve_s,
            vo_s,
            att_s,
        )
        result[m] = feed_forward(y, gains, up, down, hidden)

        for k, d in patch_order(p, n_patch, False):
            remote(
                result.at[m, at16(d)],
                back.at[s, m, p],
                result_send.at[m, k],
                back_sem.at[s, m, p],
                (s, d, h),
            )
        pltpu.make_async_copy(result.at[m, at16(p)], back.at[s, m, p], back_sem.at[s, m, p]).start()

        @pl.when(s == 1)
        def _():
            for k, d in patch_order(p, n_patch, True):
                remote(
                    result.at[m, at16(d)],
                    back.at[1, m, p],
                    final_send.at[m, k],
                    back_sem.at[1, m, p],
                    (0, d, h),
                )

    loop(0, 2, patch_step)

    def turn_back(b, m):
        loop(0, n_patch, lambda k: arrive(back.at[b, m, k], back_sem.at[b, m, k]))
        return dot(turn[...], back[b, m].reshape(256, 512)).astype(BF).reshape(16, 16, 512)

    @pl.when(s == 0)
    def _():
        def hand_step(m):
            handed[m] = turn_back(0, m)

            for k, d in hour_order(h, n_hour, True):
                remote(
                    handed.at[m, pl.ds(2 * d, 2)],
                    timed.at[m, :, at16(h)],
                    handed_send.at[m, k],
                    timed_sem.at[m, h],
                    (1, p, d),
                )

        loop(0, 2, hand_step)

    def final_step(m):
        final[m] = turn_back(1, m)
        pltpu.make_async_copy(final.at[m], out.at[m], out_sem.at[m]).start()

    loop(0, 2, final_step)

    def finish(m):
        def hours(k):
            arrive(mixed.at[m, :, at16(k)], mixed_send.at[m, k])

        def patches(k):
            arrive(turned.at[m, k], turned_send.at[m, k])
            arrive(result.at[m, at16(k)], result_send.at[m, k])

        loop(1, n_hour, hours)
        loop(0, n_patch - 1, patches)

        @pl.when(s == 0)
        def _():
            loop(0, n_hour, lambda k: arrive(handed.at[m, pl.ds(2 * k, 2)], handed_send.at[m, k]))

        @pl.when(s == 1)
        def _():
            loop(0, n_patch, lambda k: arrive(result.at[m, at16(k)], final_send.at[m, k]))

        pltpu.make_async_copy(final.at[m], out.at[m], out_sem.at[m]).wait()

    loop(0, 2, finish)
    loop(1, n_hour, lambda k: arrive(timed.at[0, :, at16(k)], in_send.at[k]))

    @pl.when(s == 1)
    def _():
        arrive(timed.at[0, :, at16(0)], in_send.at[0])


def solution(mesh):
    n_patch, n_hour = mesh.shape["patch"], mesh.shape["hour"]
    placed = (
        P(None, "patch", "hour", None),
        P(),
        P("pipe", None, None),
        P("pipe", None, None),
        P("pipe", None, None, None),
        P("pipe", None, None, None),
        P("pipe", None, None),
        P("pipe", None, None),
    )

    def local(inputs, visibility, norm_gains, scales, mixer_in, mixer_out, expand, reduce):
        tile = (256, 512)
        scratch = [
            pltpu.VMEM((2, 512, 1536), BF),
            pltpu.VMEM((2, 512, 512), BF),
            pltpu.VMEM((512, 2048), BF),
            pltpu.VMEM((2048, 512), BF),
            pltpu.VMEM((2, 2, 128, 512), BF),
            pltpu.VMEM((2, 2, 128, 512), BF),
            pltpu.VMEM((2, 16, 16, 512), BF),
            pltpu.VMEM((2, 16, 16, 512), BF),
            pltpu.VMEM((2, 256, 512), BF),
            pltpu.VMEM((2, 256, 512), BF),
            pltpu.VMEM((2, 2, 16, 16, 512), BF),
            pltpu.VMEM((2, 16, 16, 512), BF),
            pltpu.VMEM((2, 16, 16, 512), BF),
            pltpu.VMEM((256, 256), BF),
            pltpu.VMEM((256, 256), BF),
            pltpu.VMEM((256, 128), BF),
        ]
        scratch += [pltpu.VMEM(tile, BF)]
        scratch += [pltpu.VMEM((4, PB, 512), BF)] * 4
        scratch += [pltpu.VMEM(tile, BF)]
        scratch += [pltpu.VMEM((256, 2048), BF)]
        dma = pltpu.SemaphoreType.DMA
        scratch += [
            dma((4,)),
            dma((2, n_hour)),
            dma((2, n_hour)),
            dma((2, n_patch)),
            dma((2, 2, n_patch)),
            dma((2,)),
            dma((n_hour,)),
            dma((2, n_hour)),
            dma((2, n_patch)),
            dma((2, n_patch)),
            dma((2, n_patch)),
            dma((2, n_hour)),
        ]
        smem = pl.BlockSpec(memory_space=pltpu.SMEM)
        hbm = pl.BlockSpec(memory_space=pl.ANY)
        return pl.pallas_call(
            functools.partial(kernel, n_patch, n_hour),
            out_shape=jax.ShapeDtypeStruct(inputs.shape, inputs.dtype),
            in_specs=[smem, smem, pl.BlockSpec(memory_space=pltpu.VMEM)] + [hbm] * 5,
            out_specs=hbm,
            scratch_shapes=scratch,
            compiler_params=pltpu.CompilerParams(collective_id=0, has_side_effects=True),
            name="space_time_blocks",
        )(
            visibility.T,
            scales,
            jnp.transpose(norm_gains, (1, 0, 2)),
            inputs,
            mixer_in,
            mixer_out,
            expand,
            reduce,
        )

    return jax.shard_map(
        local, mesh=mesh, in_specs=placed, out_specs=P(None, "patch", "hour", None), check_vma=False
    )
```

```python
import functools
import math

import jax
import jax.numpy as jnp
from jax import lax
from jax.experimental import pallas as pl
from jax.experimental.pallas import tpu as pltpu
from jax.sharding import PartitionSpec as P

HEADS = 8
HEAD_DIM = 64
PB = 64
KV = 2
BF = jnp.bfloat16
F32 = jnp.float32
MESH = pl.DeviceIdType.MESH


def iota(shape, axis):
    return lax.broadcasted_iota(jnp.int32, shape, axis)


def dot(a, b):
    return jnp.dot(a, b, preferred_element_type=F32)


def dot_nt(a, b):
    return lax.dot_general(a, b, (((1,), (1,)), ((), ())), preferred_element_type=F32)


def rms(x, gain):
    x = x.astype(F32)
    factor = lax.rsqrt(jnp.mean(x * x, axis=-1, keepdims=True) + 1e-05)
    return (x * factor * gain).astype(BF)


def fill_constants(turn, apart, weave, same_head, pair_sums):
    r, c = iota((256, 256), 0), iota((256, 256), 1)
    turn[...] = jnp.where(c == (r % 16) * 16 + r // 16, 1.0, 0.0).astype(BF)
    apart[...] = jnp.where(c == 2 * (r % 128) + r // 128, 1.0, 0.0).astype(BF)
    weave[...] = jnp.where(c == (r % 2) * 128 + r // 2, 1.0, 0.0).astype(BF)
    same_head[...] = jnp.where(r // HEAD_DIM == c // HEAD_DIM, 1.0, 0.0).astype(BF)
    r, c = iota((256, 128), 0), iota((256, 128), 1)
    pair_sums[...] = jnp.where(r // 128 == c // HEAD_DIM, 1.0, 0.0).astype(BF)


def project(normed, which, weight_in, scales, same_head, q_s, ke_s, ko_s, ve_s, vo_s):
    width = 2 * 256
    lane = iota((1, 256), 1)
    even = (lane // HEAD_DIM) % 2 == 0
    zero = jnp.zeros((256, 256), BF)
    for part in range(3):
        for half in range(2):
            at = pl.ds(half * 256, 256)
            value = dot(normed, weight_in[which, :, pl.ds(part * width + half * 256, 256)])
            if part < 2:
                squares = dot((value * value).astype(BF), same_head[...])
                value = value * lax.rsqrt(squares * (1.0 / HEAD_DIM) + 1e-06)
            if part == 0:
                row = jnp.zeros((1, 256), F32)
                for n in range(4):
                    scale = scales[0, which, half * 4 + n] * (math.log2(math.e) / HEAD_DIM)
                    row = jnp.where(lane // HEAD_DIM == n, scale, row)
                q_s[:, at] = (value * row).astype(BF)
            else:
                even_s, odd_s = (ke_s, ko_s) if part == 1 else (ve_s, vo_s)
                value = value.astype(BF)
                even_s[:, :, at] = jnp.where(even, value, zero).reshape(4, PB, 256)
                odd_s[:, :, at] = jnp.where(even, zero, value).reshape(4, PB, 256)


def attend(queries, keys, values, pair_sums):
    weights = jnp.exp2(dot_nt(queries, keys)).astype(BF)
    mixed = dot(weights, jnp.concatenate([values, pair_sums], axis=1))
    return (mixed[:, :128] / mixed[:, 128:]).astype(BF)


def gelu(u):
    return 0.5 * u * (1.0 + jnp.tanh(math.sqrt(2.0 / math.pi) * (u + 0.044715 * (u * u * u))))


def time_stage(x, gains, scales, w_in, w_out, same_head, pair_sums, q_s, ke_s, ko_s, ve_s, vo_s, att_s):
    normed = rms(x, gains[0])
    project(normed, 0, w_in, scales, same_head, q_s, ke_s, ko_s, ve_s, vo_s)
    for a in range(2):
        rows = pl.ds(a * 128, 128)
        for j in range(4):
            at = pl.ds(j * 128, 128)
            keys = jnp.concatenate([k[2 * a + i, :, at] for k in (ke_s, ko_s) for i in range(2)], axis=0)
            values = jnp.concatenate([v[2 * a + i, :, at] for v in (ve_s, vo_s) for i in range(2)], axis=0)
            att_s[rows, at] = attend(q_s[rows, at], keys, values, pair_sums[...])
    return (x.astype(F32) + dot(att_s[...], w_out[0])).astype(BF)


def patch_stage(
    x, vis, gains, scales, w_in, w_out, same_head, pair_sums, q_s, ke_s, ko_s, ve_s, vo_s, att_s
):
    normed = rms(x, gains[1])
    project(normed, 1, w_in, scales, same_head, q_s, ke_s, ko_s, ve_s, vo_s)
    for b in range(4):
        rows = pl.ds(b * PB, PB)
        seen = [vis[i, b] for i in range(KV)]
        for j in range(4):
            at = pl.ds(j * 128, 128)
            keys = jnp.concatenate([s[z, :, at] for s in (ke_s, ko_s) for z in seen], axis=0)
            values = jnp.concatenate([s[z, :, at] for s in (ve_s, vo_s) for z in seen], axis=0)
            att_s[rows, at] = attend(q_s[rows, at], keys, values, pair_sums[...])
    return (x.astype(F32) + dot(att_s[...], w_out[1])).astype(BF)


def feed_forward(x, gains, up, down, hidden):
    normed = rms(x, gains[2])
    for c in range(8):
        at = pl.ds(c * 256, 256)
        hidden[:, at] = gelu(dot(normed, up[:, at])).astype(BF)
    return (x.astype(F32) + dot(hidden[...], down[...])).astype(BF)


def hour_order(h, n_hour, with_self):
    half = n_hour // 2
    steps = [half] + [k for i in range(half - 1, 0, -1) for k in (i, n_hour - i)] + [0] * with_self
    return [(k, lax.rem(h + k, n_hour)) for k in steps]


def patch_order(p, n_patch, with_self):
    x, y, c = p // 4, lax.rem(p // 2, 2), lax.rem(p, 2)
    steps = [(dx, dy, dc) for dy in (1, 0) for dx in (2, 1, 3, 0) for dc in (0, 1)]
    steps.sort(key=lambda t: (-(min(t[0], 4 - t[0]) + 2 * t[1]), -t[2]))
    order = []
    for k, (dx, dy, dc) in enumerate(steps):
        if (dx, dy, dc) != (0, 0, 0) or with_self:
            d = lax.rem(x + dx, n_patch // 4) * 4 + lax.rem(y + dy, 2) * 2 + lax.rem(c + dc, 2)
            order.append((k, d))
    return order


def all_order(p, h, n_patch, n_hour):
    patches = {}
    for t in [(dx, dy, dc) for dy in (1, 0) for dx in (2, 1, 3, 0) for dc in (0, 1)]:
        x, y, c = p // 4, lax.rem(p // 2, 2), lax.rem(p, 2)
        d = lax.rem(x + t[0], n_patch // 4) * 4 + lax.rem(y + t[1], 2) * 2 + lax.rem(c + t[2], 2)
        patches[t] = (min(t[0], 4 - t[0]) + 2 * t[1], d)
    hours = {k: (min(k, n_hour - k), d) for k, d in hour_order(h, n_hour, True)}
    pairs = [(hops + hop, d, e) for hops, d in patches.values() for hop, e in hours.values()]
    pairs.sort(key=lambda t: -t[0])
    return [(d, e) for hops, d, e in pairs if not (d is patches[(0, 0, 0)][1] and e is hours[0][1])]


def loop(start, stop, body):
    def step(i, carry):
        body(i)
        return carry

    lax.fori_loop(start, stop, step, 0)


def kernel(
    n_patch,
    n_hour,
    vis,
    scales,
    gains,
    inputs,
    w_in_hbm,
    w_out_hbm,
    up_hbm,
    down_hbm,
    out,
    w_in,
    w_out,
    up,
    down,
    timed,
    arrived,
    mixed,
    spread,
    handed,
    result,
    back,
    final,
    x_s,
    turn,
    apart,
    weave,
    same_head,
    pair_sums,
    q_s,
    ke_s,
    ko_s,
    ve_s,
    vo_s,
    att_s,
    hidden,
    w_sem,
    timed_sem,
    arrived_sem,
    spread_sem,
    back_sem,
    out_sem,
    in_send,
    mixed_send,
    handed_send,
    result_send,
    final_send,
):
    s = lax.axis_index("pipe")
    p = lax.axis_index("patch")
    h = lax.axis_index("hour")

    loads = [
        pltpu.make_async_copy(src.at[0], dst, w_sem.at[i])
        for i, (src, dst) in enumerate(
            [(w_in_hbm, w_in), (w_out_hbm, w_out), (up_hbm, up), (down_hbm, down)]
        )
    ]
    for load in loads:
        load.start()

    def at16(i):
        return pl.ds(pl.multiple_of(i * 16, 16), 16)

    def remote(src, dst, send, recv, device):
        pltpu.make_async_remote_copy(
            src_ref=src,
            dst_ref=dst,
            send_sem=send,
            recv_sem=recv,
            device_id=device,
            device_id_type=MESH,
        ).start()

    def arrive(ref, sem):
        pltpu.make_async_copy(ref, ref, sem).wait()

    barrier = pltpu.get_barrier_semaphore()

    def greet(device):
        pl.semaphore_signal(barrier, inc=1, device_id=device, device_id_type=MESH)

    loop(1, n_hour, lambda k: greet((s, p, lax.rem(h + k, n_hour))))
    loop(1, n_patch, lambda k: greet((s, lax.rem(p + k, n_patch), h)))
    loop(0, n_hour, lambda k: greet((1 - s, p, k)))

    fill_constants(turn, apart, weave, same_head, pair_sums)

    pl.semaphore_wait(barrier, (n_hour - 1) + (n_patch - 1) + n_hour)
    me = p * n_hour + h
    hour = h * n_patch + p

    def send_input(m, k, d):
        remote(
            inputs.at[m, pl.ds(2 * d, 2)],
            timed.at[m, :, at16(h)],
            in_send.at[k],
            timed_sem.at[m, h],
            (0, p, d),
        )

    @pl.when(s == 0)
    def _():
        for k, d in hour_order(h, n_hour, False):
            send_input(0, k, d)
        pltpu.make_async_copy(
            inputs.at[0, pl.ds(2 * h, 2)], timed.at[0, :, at16(h)], timed_sem.at[0, h]
        ).start()

    @pl.when(s == 1)
    def _():
        for k, d in hour_order(h, n_hour, True):
            send_input(1, k, d)

    loads[0].wait()
    loads[1].wait()

    def time_step(m):
        @pl.when(s == 0)
        def _():
            loop(0, n_hour, lambda k: arrive(timed.at[m, :, at16(k)], timed_sem.at[m, k]))
            x_s[...] = timed[m].reshape(256, 512)

        @pl.when(s == 1)
        def _():
            arrive(arrived.at[m], arrived_sem.at[m])
            x_s[...] = dot(apart[...], arrived[m].reshape(256, 512)).astype(BF)

        y = time_stage(
            x_s[...],
            gains,
            scales,
            w_in,
            w_out,
            same_head,
            pair_sums,
            q_s,
            ke_s,
            ko_s,
            ve_s,
            vo_s,
            att_s,
        )
        mixed[m] = dot(weave[...], y).astype(BF).reshape(128, 2, 512)
        for d, e in all_order(p, h, n_patch, n_hour):
            remote(
                mixed.at[m, e * n_patch + d],
                spread.at[m, me],
                mixed_send.at[m],
                spread_sem.at[m],
                (s, d, e),
            )
        pltpu.make_async_copy(mixed.at[m, hour], spread.at[m, me], spread_sem.at[m]).start()

    loop(0, 2, time_step)
    loads[2].wait()
    loads[3].wait()

    def patch_step(m):
        arrive(spread.at[m], spread_sem.at[m])
        y = patch_stage(
            spread[m].reshape(256, 512),
            vis,
            gains,
            scales,
            w_in,
            w_out,
            same_head,
            pair_sums,
            q_s,
            ke_s,
            ko_s,
            ve_s,
            vo_s,
            att_s,
        )
        x_s[...] = feed_forward(y, gains, up, down, hidden)

        @pl.when(s == 0)
        def _():
            handed[m] = x_s[...].reshape(128, 2, 512)
            for d, e in all_order(p, h, n_patch, n_hour) + [(p, h)]:
                remote(
                    handed.at[m, d * n_hour + e],
                    arrived.at[m, hour],
                    handed_send.at[m],
                    arrived_sem.at[m],
                    (1, d, e),
                )

        @pl.when(s == 1)
        def _():
            result[m] = x_s[...]
            for k, d in patch_order(p, n_patch, True):
                for q in (0, 1):
                    if q == 0 or k < n_patch - 1:
                        remote(
                            result.at[m, at16(d)],
                            back.at[m, p],
                            (final_send, result_send)[q].at[m, k],
                            back_sem.at[m, p],
                            (q, d, h),
                        )
            pltpu.make_async_copy(result.at[m, at16(p)], back.at[m, p], back_sem.at[m, p]).start()

    loop(0, 2, patch_step)

    def final_step(m):
        loop(0, n_patch, lambda k: arrive(back.at[m, k], back_sem.at[m, k]))
        turned = dot(turn[...], back[m].reshape(256, 512))
        final[m] = turned.astype(BF).reshape(16, 16, 512)
        pltpu.make_async_copy(final.at[m], out.at[m], out_sem.at[m]).start()

    loop(0, 2, final_step)

    def finish(m):
        others = pl.ds(0, n_patch * n_hour - 1)
        arrive(mixed.at[m, others], mixed_send.at[m])

        @pl.when(s == 0)
        def _():
            arrive(handed.at[m], handed_send.at[m])

        @pl.when(s == 1)
        def _():
            loop(0, n_patch, lambda k: arrive(result.at[m, at16(k)], final_send.at[m, k]))
            loop(0, n_patch - 1, lambda k: arrive(result.at[m, at16(k)], result_send.at[m, k]))

        pltpu.make_async_copy(final.at[m], out.at[m], out_sem.at[m]).wait()

    loop(0, 2, finish)
    loop(1, n_hour, lambda k: arrive(timed.at[0, :, at16(k)], in_send.at[k]))

    @pl.when(s == 1)
    def _():
        arrive(timed.at[0, :, at16(0)], in_send.at[0])


def solution(mesh):
    n_patch, n_hour = mesh.shape["patch"], mesh.shape["hour"]
    placed = (
        P(None, "patch", "hour", None),
        P(),
        P("pipe", None, None),
        P("pipe", None, None),
        P("pipe", None, None, None),
        P("pipe", None, None, None),
        P("pipe", None, None),
        P("pipe", None, None),
    )

    def local(inputs, visibility, norm_gains, scales, mixer_in, mixer_out, expand, reduce):
        tile = (256, 512)
        scratch = [
            pltpu.VMEM((2, 512, 1536), BF),
            pltpu.VMEM((2, 512, 512), BF),
            pltpu.VMEM((512, 2048), BF),
            pltpu.VMEM((2048, 512), BF),
            pltpu.VMEM((2, 2, 128, 512), BF),
            pltpu.VMEM((2, 128, 2, 512), BF),
            pltpu.VMEM((2, 128, 2, 512), BF),
            pltpu.VMEM((2, 128, 2, 512), BF),
            pltpu.VMEM((2, 128, 2, 512), BF),
            pltpu.VMEM((2, 256, 512), BF),
            pltpu.VMEM((2, 16, 16, 512), BF),
            pltpu.VMEM((2, 16, 16, 512), BF),
            pltpu.VMEM(tile, BF),
            pltpu.VMEM((256, 256), BF),
            pltpu.VMEM((256, 256), BF),
            pltpu.VMEM((256, 256), BF),
            pltpu.VMEM((256, 256), BF),
            pltpu.VMEM((256, 128), BF),
        ]
        scratch += [pltpu.VMEM(tile, BF)]
        scratch += [pltpu.VMEM((4, PB, 512), BF)] * 4
        scratch += [pltpu.VMEM(tile, BF)]
        scratch += [pltpu.VMEM((256, 2048), BF)]
        dma = pltpu.SemaphoreType.DMA
        scratch += [
            dma((4,)),
            dma((2, n_hour)),
            dma((2,)),
            dma((2,)),
            dma((2, n_patch)),
            dma((2,)),
            dma((n_hour,)),
            dma((2,)),
            dma((2,)),
            dma((2, n_patch)),
            dma((2, n_patch)),
        ]
        smem = pl.BlockSpec(memory_space=pltpu.SMEM)
        hbm = pl.BlockSpec(memory_space=pl.ANY)
        return pl.pallas_call(
            functools.partial(kernel, n_patch, n_hour),
            out_shape=jax.ShapeDtypeStruct(inputs.shape, inputs.dtype),
            in_specs=[smem, smem, pl.BlockSpec(memory_space=pltpu.VMEM)] + [hbm] * 5,
            out_specs=hbm,
            scratch_shapes=scratch,
            compiler_params=pltpu.CompilerParams(collective_id=0, has_side_effects=True),
            name="space_time_blocks",
        )(
            visibility.T,
            scales,
            jnp.transpose(norm_gains, (1, 0, 2)),
            inputs,
            mixer_in,
            mixer_out,
            expand,
            reduce,
        )

    return jax.shard_map(
        local, mesh=mesh, in_specs=placed, out_specs=P(None, "patch", "hour", None), check_vma=False
    )
```

```python
import functools
import math

import jax
import jax.numpy as jnp
from jax import lax
from jax.experimental import pallas as pl
from jax.experimental.pallas import tpu as pltpu
from jax.sharding import PartitionSpec as P

HEADS = 8
HEAD_DIM = 64
PB = 64
KV = 2
BF = jnp.bfloat16
F32 = jnp.float32
MESH = pl.DeviceIdType.MESH


def iota(shape, axis):
    return lax.broadcasted_iota(jnp.int32, shape, axis)


def dot(a, b):
    return jnp.dot(a, b, preferred_element_type=F32)


def dot_nt(a, b):
    return lax.dot_general(a, b, (((1,), (1,)), ((), ())), preferred_element_type=F32)


def rms(x, gain):
    x = x.astype(F32)
    factor = lax.rsqrt(jnp.mean(x * x, axis=-1, keepdims=True) + 1e-05)
    return (x * factor * gain).astype(BF)


def fill_constants(apart, weave, same_head, pair_sums):
    r, c = iota((256, 256), 0), iota((256, 256), 1)
    apart[...] = jnp.where(c == 2 * (r % 128) + r // 128, 1.0, 0.0).astype(BF)
    weave[...] = jnp.where(c == (r % 2) * 128 + r // 2, 1.0, 0.0).astype(BF)
    same_head[...] = jnp.where(r // HEAD_DIM == c // HEAD_DIM, 1.0, 0.0).astype(BF)
    r, c = iota((256, 128), 0), iota((256, 128), 1)
    pair_sums[...] = jnp.where(r // 128 == c // HEAD_DIM, 1.0, 0.0).astype(BF)


def project(normed, which, weight_in, scales, same_head, q_s, ke_s, ko_s, ve_s, vo_s):
    width = 2 * 256
    lane = iota((1, 256), 1)
    even = (lane // HEAD_DIM) % 2 == 0
    zero = jnp.zeros((256, 256), BF)
    for part in range(3):
        for half in range(2):
            at = pl.ds(half * 256, 256)
            value = dot(normed, weight_in[which, :, pl.ds(part * width + half * 256, 256)])
            if part < 2:
                squares = dot((value * value).astype(BF), same_head[...])
                value = value * lax.rsqrt(squares * (1.0 / HEAD_DIM) + 1e-06)
            if part == 0:
                row = jnp.zeros((1, 256), F32)
                for n in range(4):
                    scale = scales[0, which, half * 4 + n] * (math.log2(math.e) / HEAD_DIM)
                    row = jnp.where(lane // HEAD_DIM == n, scale, row)
                q_s[:, at] = (value * row).astype(BF)
            else:
                even_s, odd_s = (ke_s, ko_s) if part == 1 else (ve_s, vo_s)
                value = value.astype(BF)
                even_s[:, :, at] = jnp.where(even, value, zero).reshape(4, PB, 256)
                odd_s[:, :, at] = jnp.where(even, zero, value).reshape(4, PB, 256)


def attend(queries, keys, values, pair_sums):
    weights = jnp.exp2(dot_nt(queries, keys)).astype(BF)
    mixed = dot(weights, jnp.concatenate([values, pair_sums], axis=1))
    return (mixed[:, :128] / mixed[:, 128:]).astype(BF)


def gelu(u):
    return 0.5 * u * (1.0 + jnp.tanh(math.sqrt(2.0 / math.pi) * (u + 0.044715 * (u * u * u))))


def time_stage(x, gains, scales, w_in, w_out, same_head, pair_sums, q_s, ke_s, ko_s, ve_s, vo_s, att_s):
    normed = rms(x, gains[0])
    project(normed, 0, w_in, scales, same_head, q_s, ke_s, ko_s, ve_s, vo_s)
    for a in range(2):
        rows = pl.ds(a * 128, 128)
        for j in range(4):
            at = pl.ds(j * 128, 128)
            keys = jnp.concatenate([k[2 * a + i, :, at] for k in (ke_s, ko_s) for i in range(2)], axis=0)
            values = jnp.concatenate([v[2 * a + i, :, at] for v in (ve_s, vo_s) for i in range(2)], axis=0)
            att_s[rows, at] = attend(q_s[rows, at], keys, values, pair_sums[...])
    return (x.astype(F32) + dot(att_s[...], w_out[0])).astype(BF)


def patch_stage(
    x, vis, gains, scales, w_in, w_out, same_head, pair_sums, q_s, ke_s, ko_s, ve_s, vo_s, att_s
):
    normed = rms(x, gains[1])
    project(normed, 1, w_in, scales, same_head, q_s, ke_s, ko_s, ve_s, vo_s)
    for b in range(4):
        rows = pl.ds(b * PB, PB)
        seen = [vis[i, b] for i in range(KV)]
        for j in range(4):
            at = pl.ds(j * 128, 128)
            keys = jnp.concatenate([s[z, :, at] for s in (ke_s, ko_s) for z in seen], axis=0)
            values = jnp.concatenate([s[z, :, at] for s in (ve_s, vo_s) for z in seen], axis=0)
            att_s[rows, at] = attend(q_s[rows, at], keys, values, pair_sums[...])
    return (x.astype(F32) + dot(att_s[...], w_out[1])).astype(BF)


def feed_forward(x, gains, up, down, hidden):
    normed = rms(x, gains[2])
    for c in range(8):
        at = pl.ds(c * 256, 256)
        hidden[:, at] = gelu(dot(normed, up[:, at])).astype(BF)
    return (x.astype(F32) + dot(hidden[...], down[...])).astype(BF)


def hour_order(h, n_hour, with_self):
    half = n_hour // 2
    steps = [half] + [k for i in range(half - 1, 0, -1) for k in (i, n_hour - i)] + [0] * with_self
    return [(k, lax.rem(h + k, n_hour)) for k in steps]


def patch_order(p, n_patch, with_self):
    x, y, c = p // 4, lax.rem(p // 2, 2), lax.rem(p, 2)
    steps = [(dx, dy, dc) for dy in (1, 0) for dx in (2, 1, 3, 0) for dc in (0, 1)]
    steps.sort(key=lambda t: (-(min(t[0], 4 - t[0]) + 2 * t[1]), -t[2]))
    order = []
    for k, (dx, dy, dc) in enumerate(steps):
        if (dx, dy, dc) != (0, 0, 0) or with_self:
            d = lax.rem(x + dx, n_patch // 4) * 4 + lax.rem(y + dy, 2) * 2 + lax.rem(c + dc, 2)
            order.append((k, d))
    return order


def all_order(p, h, n_patch, n_hour):
    patches = {}
    for t in [(dx, dy, dc) for dy in (1, 0) for dx in (2, 1, 3, 0) for dc in (0, 1)]:
        x, y, c = p // 4, lax.rem(p // 2, 2), lax.rem(p, 2)
        d = lax.rem(x + t[0], n_patch // 4) * 4 + lax.rem(y + t[1], 2) * 2 + lax.rem(c + t[2], 2)
        patches[t] = (min(t[0], 4 - t[0]) + 2 * t[1], d)
    hours = {k: (min(k, n_hour - k), d) for k, d in hour_order(h, n_hour, True)}
    pairs = [(hops + hop, d, e) for hops, d in patches.values() for hop, e in hours.values()]
    pairs.sort(key=lambda t: -t[0])
    return [(d, e) for hops, d, e in pairs if not (d is patches[(0, 0, 0)][1] and e is hours[0][1])]


def loop(start, stop, body):
    def step(i, carry):
        body(i)
        return carry

    lax.fori_loop(start, stop, step, 0)


def kernel(
    n_patch,
    n_hour,
    vis,
    scales,
    gains,
    inputs,
    w_in_hbm,
    w_out_hbm,
    up_hbm,
    down_hbm,
    out,
    w_in,
    w_out,
    up,
    down,
    timed,
    arrived,
    mixed,
    spread,
    handed,
    result,
    x_s,
    apart,
    weave,
    same_head,
    pair_sums,
    q_s,
    ke_s,
    ko_s,
    ve_s,
    vo_s,
    att_s,
    hidden,
    w_sem,
    timed_sem,
    arrived_sem,
    spread_sem,
    back_sem,
    in_send,
    mixed_send,
    handed_send,
    result_send,
    final_send,
):
    s = lax.axis_index("pipe")
    p = lax.axis_index("patch")
    h = lax.axis_index("hour")

    loads = [
        pltpu.make_async_copy(src.at[0], dst, w_sem.at[i])
        for i, (src, dst) in enumerate(
            [(w_in_hbm, w_in), (w_out_hbm, w_out), (up_hbm, up), (down_hbm, down)]
        )
    ]
    for load in loads:
        load.start()

    def at16(i):
        return pl.ds(pl.multiple_of(i * 16, 16), 16)

    def remote(src, dst, send, recv, device):
        pltpu.make_async_remote_copy(
            src_ref=src,
            dst_ref=dst,
            send_sem=send,
            recv_sem=recv,
            device_id=device,
            device_id_type=MESH,
        ).start()

    def arrive(ref, sem):
        pltpu.make_async_copy(ref, ref, sem).wait()

    barrier = pltpu.get_barrier_semaphore()

    def greet(device):
        pl.semaphore_signal(barrier, inc=1, device_id=device, device_id_type=MESH)

    loop(1, n_hour, lambda k: greet((s, p, lax.rem(h + k, n_hour))))
    loop(1, n_patch, lambda k: greet((s, lax.rem(p + k, n_patch), h)))
    loop(0, n_hour, lambda k: greet((1 - s, p, k)))

    fill_constants(apart, weave, same_head, pair_sums)

    pl.semaphore_wait(barrier, (n_hour - 1) + (n_patch - 1) + n_hour)
    me = p * n_hour + h
    hour = h * n_patch + p

    for m in range(2):
        own = (inputs.at[m, 2 * h + s], timed.at[m, s, at16(h)])
        for k, d in hour_order(h, n_hour, False):
            remote(
                inputs.at[m, 2 * d + s], own[1], in_send.at[m, k], timed_sem.at[m, s, h], (0, p, d)
            )

        @pl.when(s == 0)
        def _(m=m, own=own):
            pltpu.make_async_copy(*own, timed_sem.at[m, 0, h]).start()

        @pl.when(s == 1)
        def _(m=m, own=own):
            remote(*own, in_send.at[m, 0], timed_sem.at[m, 1, h], (0, p, h))

    loads[0].wait()
    loads[1].wait()

    def time_step(m):
        @pl.when(s == 0)
        def _():
            for a in range(2):
                loop(0, n_hour, lambda k: arrive(timed.at[m, a, at16(k)], timed_sem.at[m, a, k]))

            x_s[...] = timed[m].reshape(256, 512)

        @pl.when(s == 1)
        def _():
            arrive(arrived.at[m], arrived_sem.at[m])
            x_s[...] = dot(apart[...], arrived[m].reshape(256, 512)).astype(BF)

        y = time_stage(
            x_s[...],
            gains,
            scales,
            w_in,
            w_out,
            same_head,
            pair_sums,
            q_s,
            ke_s,
            ko_s,
            ve_s,
            vo_s,
            att_s,
        )
        mixed[m] = dot(weave[...], y).astype(BF).reshape(128, 2, 512)
        for d, e in all_order(p, h, n_patch, n_hour):
            remote(
                mixed.at[m, e * n_patch + d],
                spread.at[m, me],
                mixed_send.at[m],
                spread_sem.at[m],
                (s, d, e),
            )
        pltpu.make_async_copy(mixed.at[m, hour], spread.at[m, me], spread_sem.at[m]).start()

    loop(0, 2, time_step)
    loads[2].wait()
    loads[3].wait()

    def patch_step(m):
        arrive(spread.at[m], spread_sem.at[m])
        y = patch_stage(
            spread[m].reshape(256, 512),
            vis,
            gains,
            scales,
            w_in,
            w_out,
            same_head,
            pair_sums,
            q_s,
            ke_s,
            ko_s,
            ve_s,
            vo_s,
            att_s,
        )
        x_s[...] = feed_forward(y, gains, up, down, hidden)

        @pl.when(s == 0)
        def _():
            handed[m] = x_s[...].reshape(128, 2, 512)
            for d, e in all_order(p, h, n_patch, n_hour) + [(p, h)]:
                remote(
                    handed.at[m, d * n_hour + e],
                    arrived.at[m, hour],
                    handed_send.at[m],
                    arrived_sem.at[m],
                    (1, d, e),
                )

        @pl.when(s == 1)
        def _():
            result[m] = x_s[...]
            for k, d in patch_order(p, n_patch, True):
                for q in (0, 1):
                    if q == 0 or k < n_patch - 1:
                        remote(
                            result.at[m, at16(d)],
                            out.at[m, p],
                            (final_send, result_send)[q].at[m, k],
                            back_sem.at[m, p],
                            (q, d, h),
                        )
            pltpu.make_async_copy(result.at[m, at16(p)], out.at[m, p], back_sem.at[m, p]).start()

    loop(0, 2, patch_step)

    def finish(m):
        others = pl.ds(0, n_patch * n_hour - 1)
        arrive(mixed.at[m, others], mixed_send.at[m])
        loop(1, n_hour, lambda k: arrive(timed.at[0, 0, at16(k)], in_send.at[m, k]))

        @pl.when(s == 0)
        def _():
            arrive(handed.at[m], handed_send.at[m])

        @pl.when(s == 1)
        def _():
            arrive(timed.at[0, 0, at16(0)], in_send.at[m, 0])
            loop(0, n_patch, lambda k: arrive(result.at[m, at16(k)], final_send.at[m, k]))
            loop(0, n_patch - 1, lambda k: arrive(result.at[m, at16(k)], result_send.at[m, k]))

        loop(0, n_patch, lambda k: arrive(out.at[m, k], back_sem.at[m, k]))

    loop(0, 2, finish)


def solution(mesh):
    n_patch, n_hour = mesh.shape["patch"], mesh.shape["hour"]
    placed = (
        P(None, "patch", "hour", None),
        P(),
        P("pipe", None, None),
        P("pipe", None, None),
        P("pipe", None, None, None),
        P("pipe", None, None, None),
        P("pipe", None, None),
        P("pipe", None, None),
    )

    def local(inputs, visibility, norm_gains, scales, mixer_in, mixer_out, expand, reduce):
        tile = (256, 512)
        scratch = [
            pltpu.VMEM((2, 512, 1536), BF),
            pltpu.VMEM((2, 512, 512), BF),
            pltpu.VMEM((512, 2048), BF),
            pltpu.VMEM((2048, 512), BF),
            pltpu.VMEM((2, 2, 128, 512), BF),
            pltpu.VMEM((2, 128, 2, 512), BF),
            pltpu.VMEM((2, 128, 2, 512), BF),
            pltpu.VMEM((2, 128, 2, 512), BF),
            pltpu.VMEM((2, 128, 2, 512), BF),
            pltpu.VMEM((2, 256, 512), BF),
            pltpu.VMEM(tile, BF),
            pltpu.VMEM((256, 256), BF),
            pltpu.VMEM((256, 256), BF),
            pltpu.VMEM((256, 256), BF),
            pltpu.VMEM((256, 128), BF),
        ]
        scratch += [pltpu.VMEM(tile, BF)]
        scratch += [pltpu.VMEM((4, PB, 512), BF)] * 4
        scratch += [pltpu.VMEM(tile, BF)]
        scratch += [pltpu.VMEM((256, 2048), BF)]
        dma = pltpu.SemaphoreType.DMA
        scratch += [
            dma((4,)),
            dma((2, 2, n_hour)),
            dma((2,)),
            dma((2,)),
            dma((2, n_patch)),
            dma((2, n_hour)),
            dma((2,)),
            dma((2,)),
            dma((2, n_patch)),
            dma((2, n_patch)),
        ]
        smem = pl.BlockSpec(memory_space=pltpu.SMEM)
        hbm = pl.BlockSpec(memory_space=pl.ANY)
        by_hour = pl.pallas_call(
            functools.partial(kernel, n_patch, n_hour),
            out_shape=jax.ShapeDtypeStruct(inputs.shape, inputs.dtype),
            in_specs=[smem, smem, pl.BlockSpec(memory_space=pltpu.VMEM)] + [hbm] * 5,
            out_specs=hbm,
            scratch_shapes=scratch,
            compiler_params=pltpu.CompilerParams(collective_id=0, has_side_effects=True),
            name="space_time_blocks",
        )(
            visibility.T,
            scales,
            jnp.transpose(norm_gains, (1, 0, 2)),
            inputs,
            mixer_in,
            mixer_out,
            expand,
            reduce,
        )
        return jnp.swapaxes(by_hour, 1, 2)

    return jax.shard_map(
        local, mesh=mesh, in_specs=placed, out_specs=P(None, "patch", "hour", None), check_vma=False
    )
```

```python
import functools
import math

import jax
import jax.numpy as jnp
from jax import lax
from jax.experimental import pallas as pl
from jax.experimental.pallas import tpu as pltpu
from jax.sharding import PartitionSpec as P

HEADS = 8
HEAD_DIM = 64
PB = 64
KV = 2
BF = jnp.bfloat16
F32 = jnp.float32
MESH = pl.DeviceIdType.MESH


def iota(shape, axis):
    return lax.broadcasted_iota(jnp.int32, shape, axis)


def dot(a, b):
    return jnp.dot(a, b, preferred_element_type=F32)


def dot_nt(a, b):
    return lax.dot_general(a, b, (((1,), (1,)), ((), ())), preferred_element_type=F32)


def rms(x, gain):
    x = x.astype(F32)
    factor = lax.rsqrt(jnp.mean(x * x, axis=-1, keepdims=True) + 1e-05)
    return (x * factor * gain).astype(BF)


def fill_constants(apart, weave, same_head, pair_sums):
    r, c = iota((256, 256), 0), iota((256, 256), 1)
    apart[...] = jnp.where(c == 2 * (r % 128) + r // 128, 1.0, 0.0).astype(BF)
    weave[...] = jnp.where(c == (r % 2) * 128 + r // 2, 1.0, 0.0).astype(BF)
    same_head[...] = jnp.where(r // HEAD_DIM == c // HEAD_DIM, 1.0 / HEAD_DIM, 0.0).astype(BF)
    r, c = iota((256, 128), 0), iota((256, 128), 1)
    pair_sums[...] = jnp.where(r // 128 == c // HEAD_DIM, 1.0, 0.0).astype(BF)


def project(normed, which, weight_in, scales, same_head, q_s, ke_s, ko_s, ve_s, vo_s, proj_s):
    width = 2 * 256
    lane = iota((1, 256), 1)
    even = (lane // HEAD_DIM) % 2 == 0
    zero = jnp.zeros((256, 256), BF)
    for part in range(6):
        proj_s[:, part * 256 : part * 256 + 256] = dot(
            normed, weight_in[which, :, pl.ds(part * 256, 256)]
        )
    for part in range(3):
        for half in range(2):
            at = pl.ds(half * 256, 256)
            value = proj_s[:, pl.ds(part * width + half * 256, 256)]
            if part < 2:
                square = dot((value * value).astype(BF), same_head[...])
                value = value * lax.rsqrt(square + 1e-06)
            if part == 0:
                row = jnp.zeros((1, 256), F32)
                for n in range(4):
                    scale = scales[0, which, half * 4 + n] * (math.log2(math.e) / HEAD_DIM)
                    row = jnp.where(lane // HEAD_DIM == n, scale, row)
                q_s[:, at] = (value * row).astype(BF)
            elif which == 1:
                (ke_s if part == 1 else ve_s)[:, :, at] = value.astype(BF).reshape(4, PB, 256)
            else:
                even_s, odd_s = (ke_s, ko_s) if part == 1 else (ve_s, vo_s)
                value = value.astype(BF)
                even_s[:, :, at] = jnp.where(even, value, zero).reshape(4, PB, 256)
                odd_s[:, :, at] = jnp.where(even, zero, value).reshape(4, PB, 256)


def twice_gelu(u):
    root = math.sqrt(2.0 / math.pi)
    return u + u * jnp.tanh(u * (root + (root * 0.044715) * (u * u)))


def time_stage(x, gains, scales, w_in, w_out, same_head, pair_sums, q_s, ke_s, ko_s, ve_s, vo_s, att_s, proj_s, weigh_s):
    normed = rms(x, gains[0])
    project(normed, 0, w_in, scales, same_head, q_s, ke_s, ko_s, ve_s, vo_s, proj_s)
    for a in range(2):
        rows = pl.ds(a * 128, 128)
        for j in range(4):
            at = pl.ds(j * 128, 128)
            keys = jnp.concatenate([k[2 * a + i, :, at] for k in (ke_s, ko_s) for i in range(2)], axis=0)
            weigh_s[:, pl.ds((a * 4 + j) * 256, 256)] = jnp.exp2(dot_nt(q_s[rows, at], keys)).astype(BF)
    for a in range(2):
        rows = pl.ds(a * 128, 128)
        for j in range(4):
            at = pl.ds(j * 128, 128)
            values = jnp.concatenate([v[2 * a + i, :, at] for v in (ve_s, vo_s) for i in range(2)], axis=0)
            mixed = dot(
                weigh_s[:, pl.ds((a * 4 + j) * 256, 256)],
                jnp.concatenate([values, pair_sums[...]], axis=1),
            )
            att_s[rows, at] = (mixed[:, :128] / mixed[:, 128:]).astype(BF)
    return (x.astype(F32) + dot(att_s[...], w_out[0])).astype(BF)


def patch_stage(
    x, vis, gains, scales, w_in, w_out, same_head, pair_sums, q_s, ke_s, ko_s, ve_s, vo_s, att_s, proj_s, weigh_s
):
    normed = rms(x, gains[1])
    project(normed, 1, w_in, scales, same_head, q_s, ke_s, ko_s, ve_s, vo_s, proj_s)
    even = iota((1, 128), 1) < HEAD_DIM
    even_pair = iota((1, 256), 1) % 128 < HEAD_DIM
    zero = jnp.zeros((PB, 128), BF)
    ones = jnp.ones((128, 128), BF)
    for b in range(4):
        rows = pl.ds(b * PB, PB)
        seen = [vis[i, b] for i in range(KV)]
        for j in range(4):
            at = pl.ds(j * 128, 128)
            keys = jnp.concatenate([ke_s[z, :, at] for z in seen], axis=0)
            queries = q_s[rows, at]
            queries = jnp.concatenate(
                [jnp.where(even, queries, zero), jnp.where(even, zero, queries)], axis=0
            )
            weigh_s[:, pl.ds((b * 4 + j) * 128, 128)] = jnp.exp2(dot_nt(queries, keys)).astype(BF)
    for b in range(4):
        rows = pl.ds(b * PB, PB)
        seen = [vis[i, b] for i in range(KV)]
        for j in range(4):
            at = pl.ds(j * 128, 128)
            values = jnp.concatenate([ve_s[z, :, at] for z in seen], axis=0)
            mixed = dot(
                weigh_s[:, pl.ds((b * 4 + j) * 128, 128)], jnp.concatenate([values, ones], axis=1)
            )
            mixed = jnp.where(even_pair, mixed[:PB], mixed[PB:])
            att_s[rows, at] = (mixed[:, :128] / mixed[:, 128:]).astype(BF)
    return (x.astype(F32) + dot(att_s[...], w_out[1])).astype(BF)


def feed_forward(x, gains, up, down, hidden, proj_s):
    normed = rms(x, gains[2])
    for part in range(2):
        for c in range(4):
            at = pl.ds(c * 256, 256)
            proj_s[:, at] = dot(normed, up[:, pl.ds(part * 1024 + c * 256, 256)])
        for c in range(4):
            at = pl.ds(c * 256, 256)
            hidden[:, pl.ds(part * 1024 + c * 256, 256)] = twice_gelu(proj_s[:, at]).astype(BF)
    return (x.astype(F32) + 0.5 * dot(hidden[...], down[...])).astype(BF)


def hour_order(h, n_hour, with_self):
    half = n_hour // 2
    steps = [half] + [k for i in range(half - 1, 0, -1) for k in (i, n_hour - i)] + [0] * with_self
    return [(k, lax.rem(h + k, n_hour)) for k in steps]


def patch_order(p, n_patch, with_self):
    x, y, c = p // 4, lax.rem(p // 2, 2), lax.rem(p, 2)
    steps = [(dx, dy, dc) for dy in (1, 0) for dx in (2, 1, 3, 0) for dc in (0, 1)]
    steps.sort(key=lambda t: (-(min(t[0], 4 - t[0]) + 2 * t[1]), -t[2]))
    order = []
    for k, (dx, dy, dc) in enumerate(steps):
        if (dx, dy, dc) != (0, 0, 0) or with_self:
            d = lax.rem(x + dx, n_patch // 4) * 4 + lax.rem(y + dy, 2) * 2 + lax.rem(c + dc, 2)
            order.append((k, d))
    return order


def all_order(p, h, n_patch, n_hour):
    patches = {}
    for t in [(dx, dy, dc) for dy in (1, 0) for dx in (2, 1, 3, 0) for dc in (0, 1)]:
        x, y, c = p // 4, lax.rem(p // 2, 2), lax.rem(p, 2)
        d = lax.rem(x + t[0], n_patch // 4) * 4 + lax.rem(y + t[1], 2) * 2 + lax.rem(c + t[2], 2)
        patches[t] = (min(t[0], 4 - t[0]) + 2 * t[1], d)
    hours = {k: (min(k, n_hour - k), d) for k, d in hour_order(h, n_hour, True)}
    pairs = [(hops + hop, d, e) for hops, d in patches.values() for hop, e in hours.values()]
    pairs.sort(key=lambda t: -t[0])
    return [(d, e) for hops, d, e in pairs if not (d is patches[(0, 0, 0)][1] and e is hours[0][1])]


def loop(start, stop, body):
    def step(i, carry):
        body(i)
        return carry

    lax.fori_loop(start, stop, step, 0)


def kernel(
    n_patch,
    n_hour,
    vis,
    scales,
    gains,
    inputs,
    w_in_hbm,
    w_out_hbm,
    up_hbm,
    down_hbm,
    out,
    w_in,
    w_out,
    up,
    down,
    timed,
    arrived,
    mixed,
    spread,
    handed,
    result,
    x_s,
    apart,
    weave,
    same_head,
    pair_sums,
    q_s,
    ke_s,
    ko_s,
    ve_s,
    vo_s,
    att_s,
    proj_s,
    weigh_s,
    hidden,
    w_sem,
    timed_sem,
    arrived_sem,
    spread_sem,
    back_sem,
    in_send,
    mixed_send,
    handed_send,
    result_send,
    final_send,
):
    s = lax.axis_index("pipe")
    p = lax.axis_index("patch")
    h = lax.axis_index("hour")

    loads = [
        pltpu.make_async_copy(src.at[0], dst, w_sem.at[i])
        for i, (src, dst) in enumerate(
            [(w_in_hbm, w_in), (w_out_hbm, w_out), (up_hbm, up), (down_hbm, down)]
        )
    ]
    for load in loads:
        load.start()

    def at16(i):
        return pl.ds(pl.multiple_of(i * 16, 16), 16)

    def remote(src, dst, send, recv, device):
        pltpu.make_async_remote_copy(
            src_ref=src,
            dst_ref=dst,
            send_sem=send,
            recv_sem=recv,
            device_id=device,
            device_id_type=MESH,
        ).start()

    def arrive(ref, sem):
        pltpu.make_async_copy(ref, ref, sem).wait()

    barrier = pltpu.get_barrier_semaphore()

    def greet(device):
        pl.semaphore_signal(barrier, inc=1, device_id=device, device_id_type=MESH)

    loop(1, n_hour, lambda k: greet((s, p, lax.rem(h + k, n_hour))))
    loop(1, n_patch, lambda k: greet((s, lax.rem(p + k, n_patch), h)))
    loop(0, n_hour, lambda k: greet((1 - s, p, k)))

    fill_constants(apart, weave, same_head, pair_sums)

    pl.semaphore_wait(barrier, (n_hour - 1) + (n_patch - 1) + n_hour)
    me = p * n_hour + h
    hour = h * n_patch + p

    for m in range(2):
        own = (inputs.at[m, 2 * h + s], timed.at[m, s, at16(h)])
        for k, d in hour_order(h, n_hour, False):
            remote(
                inputs.at[m, 2 * d + s], own[1], in_send.at[m, k], timed_sem.at[m, s, h], (0, p, d)
            )

        @pl.when(s == 0)
        def _(m=m, own=own):
            pltpu.make_async_copy(*own, timed_sem.at[m, 0, h]).start()

        @pl.when(s == 1)
        def _(m=m, own=own):
            remote(*own, in_send.at[m, 0], timed_sem.at[m, 1, h], (0, p, h))

    loads[0].wait()
    loads[1].wait()

    def time_step(m):
        @pl.when(s == 0)
        def _():
            for a in range(2):
                loop(0, n_hour, lambda k: arrive(timed.at[m, a, at16(k)], timed_sem.at[m, a, k]))

            x_s[...] = timed[m].reshape(256, 512)

        @pl.when(s == 1)
        def _():
            arrive(arrived.at[m], arrived_sem.at[m])
            x_s[...] = dot(apart[...], arrived[m].reshape(256, 512)).astype(BF)

        y = time_stage(
            x_s[...],
            gains,
            scales,
            w_in,
            w_out,
            same_head,
            pair_sums,
            q_s,
            ke_s,
            ko_s,
            ve_s,
            vo_s,
            att_s,
            proj_s,
            weigh_s,
        )
        mixed[m] = dot(weave[...], y).astype(BF).reshape(128, 2, 512)
        for d, e in all_order(p, h, n_patch, n_hour):
            remote(
                mixed.at[m, e * n_patch + d],
                spread.at[m, me],
                mixed_send.at[m],
                spread_sem.at[m],
                (s, d, e),
            )
        pltpu.make_async_copy(mixed.at[m, hour], spread.at[m, me], spread_sem.at[m]).start()

    loop(0, 2, time_step)
    loads[2].wait()
    loads[3].wait()

    def patch_step(m):
        arrive(spread.at[m], spread_sem.at[m])
        y = patch_stage(
            spread[m].reshape(256, 512),
            vis,
            gains,
            scales,
            w_in,
            w_out,
            same_head,
            pair_sums,
            q_s,
            ke_s,
            ko_s,
            ve_s,
            vo_s,
            att_s,
            proj_s,
            weigh_s,
        )
        x_s[...] = feed_forward(y, gains, up, down, hidden, proj_s)

        @pl.when(s == 0)
        def _():
            handed[m] = x_s[...].reshape(128, 2, 512)
            for d, e in all_order(p, h, n_patch, n_hour) + [(p, h)]:
                remote(
                    handed.at[m, d * n_hour + e],
                    arrived.at[m, hour],
                    handed_send.at[m],
                    arrived_sem.at[m],
                    (1, d, e),
                )

        @pl.when(s == 1)
        def _():
            result[m] = x_s[...]
            for k, d in patch_order(p, n_patch, True):
                for q in (0, 1):
                    if q == 0 or k < n_patch - 1:
                        remote(
                            result.at[m, at16(d)],
                            out.at[m, p],
                            (final_send, result_send)[q].at[m, k],
                            back_sem.at[m, p],
                            (q, d, h),
                        )
            pltpu.make_async_copy(result.at[m, at16(p)], out.at[m, p], back_sem.at[m, p]).start()

    loop(0, 2, patch_step)

    def finish(m):
        others = pl.ds(0, n_patch * n_hour - 1)
        arrive(mixed.at[m, others], mixed_send.at[m])
        loop(1, n_hour, lambda k: arrive(timed.at[0, 0, at16(k)], in_send.at[m, k]))

        @pl.when(s == 0)
        def _():
            arrive(handed.at[m], handed_send.at[m])

        @pl.when(s == 1)
        def _():
            arrive(timed.at[0, 0, at16(0)], in_send.at[m, 0])
            loop(0, n_patch, lambda k: arrive(result.at[m, at16(k)], final_send.at[m, k]))
            loop(0, n_patch - 1, lambda k: arrive(result.at[m, at16(k)], result_send.at[m, k]))

        loop(0, n_patch, lambda k: arrive(out.at[m, k], back_sem.at[m, k]))

    loop(0, 2, finish)


def solution(mesh):
    n_patch, n_hour = mesh.shape["patch"], mesh.shape["hour"]
    placed = (
        P(None, "patch", "hour", None),
        P(),
        P("pipe", None, None),
        P("pipe", None, None),
        P("pipe", None, None, None),
        P("pipe", None, None, None),
        P("pipe", None, None),
        P("pipe", None, None),
    )

    def local(inputs, visibility, norm_gains, scales, mixer_in, mixer_out, expand, reduce):
        tile = (256, 512)
        scratch = [
            pltpu.VMEM((2, 512, 1536), BF),
            pltpu.VMEM((2, 512, 512), BF),
            pltpu.VMEM((512, 2048), BF),
            pltpu.VMEM((2048, 512), BF),
            pltpu.VMEM((2, 2, 128, 512), BF),
            pltpu.VMEM((2, 128, 2, 512), BF),
            pltpu.VMEM((2, 128, 2, 512), BF),
            pltpu.VMEM((2, 128, 2, 512), BF),
            pltpu.VMEM((2, 128, 2, 512), BF),
            pltpu.VMEM((2, 256, 512), BF),
            pltpu.VMEM(tile, BF),
            pltpu.VMEM((256, 256), BF),
            pltpu.VMEM((256, 256), BF),
            pltpu.VMEM((256, 256), BF),
            pltpu.VMEM((256, 128), BF),
        ]
        scratch += [pltpu.VMEM(tile, BF)]
        scratch += [pltpu.VMEM((4, PB, 512), BF)] * 4
        scratch += [pltpu.VMEM(tile, BF)]
        scratch += [pltpu.VMEM((256, 1536), F32)]
        scratch += [pltpu.VMEM((128, 2048), BF)]
        scratch += [pltpu.VMEM((256, 2048), BF)]
        dma = pltpu.SemaphoreType.DMA
        scratch += [
            dma((4,)),
            dma((2, 2, n_hour)),
            dma((2,)),
            dma((2,)),
            dma((2, n_patch)),
            dma((2, n_hour)),
            dma((2,)),
            dma((2,)),
            dma((2, n_patch)),
            dma((2, n_patch)),
        ]
        smem = pl.BlockSpec(memory_space=pltpu.SMEM)
        hbm = pl.BlockSpec(memory_space=pl.ANY)
        by_hour = pl.pallas_call(
            functools.partial(kernel, n_patch, n_hour),
            out_shape=jax.ShapeDtypeStruct(inputs.shape, inputs.dtype),
            in_specs=[smem, smem, pl.BlockSpec(memory_space=pltpu.VMEM)] + [hbm] * 5,
            out_specs=hbm,
            scratch_shapes=scratch,
            compiler_params=pltpu.CompilerParams(collective_id=0, has_side_effects=True),
            name="space_time_blocks",
        )(
            visibility.T,
            scales,
            jnp.transpose(norm_gains, (1, 0, 2)),
            inputs,
            mixer_in,
            mixer_out,
            expand,
            reduce,
        )
        return jnp.swapaxes(by_hour, 1, 2)

    return jax.shard_map(
        local, mesh=mesh, in_specs=placed, out_specs=P(None, "patch", "hour", None), check_vma=False
    )
```

```python
import functools
import math

import jax
import jax.numpy as jnp
from jax import lax
from jax.experimental import pallas as pl
from jax.experimental.pallas import tpu as pltpu
from jax.sharding import PartitionSpec as P

HEADS = 8
HEAD_DIM = 64
PB = 64
KV = 2
BF = jnp.bfloat16
F32 = jnp.float32
MESH = pl.DeviceIdType.MESH


def iota(shape, axis):
    return lax.broadcasted_iota(jnp.int32, shape, axis)


def dot(a, b):
    return jnp.dot(a, b, preferred_element_type=F32)


def dot_nt(a, b):
    return lax.dot_general(a, b, (((1,), (1,)), ((), ())), preferred_element_type=F32)


def rms(x, gain):
    x = x.astype(F32)
    factor = lax.rsqrt(jnp.mean(x * x, axis=-1, keepdims=True) + 1e-05)
    return (x * gain).astype(BF), factor


def fill_constants(apart, weave, same_head, pair_sums):
    r, c = iota((256, 256), 0), iota((256, 256), 1)
    apart[...] = jnp.where(c == 2 * (r % 128) + r // 128, 1.0, 0.0).astype(BF)
    weave[...] = jnp.where(c == (r % 2) * 128 + r // 2, 1.0, 0.0).astype(BF)
    same_head[...] = jnp.where(r // HEAD_DIM == c // HEAD_DIM, 1.0 / HEAD_DIM, 0.0).astype(BF)
    r, c = iota((256, 128), 0), iota((256, 128), 1)
    pair_sums[...] = jnp.where(r // 128 == c // HEAD_DIM, 1.0, 0.0).astype(BF)


def project(normed, factor, which, weight_in, scales, same_head, q_s, ke_s, ko_s, ve_s, vo_s, proj_s):
    width = 2 * 256
    lane = iota((1, 256), 1)
    even = (lane // HEAD_DIM) % 2 == 0
    zero = jnp.zeros((256, 256), BF)

    def put(even_s, odd_s, at, value):
        value = value.astype(BF)
        if which == 1:
            even_s[:, :, at] = value.reshape(4, PB, 256)
        else:
            even_s[:, :, at] = jnp.where(even, value, zero).reshape(4, PB, 256)
            odd_s[:, :, at] = jnp.where(even, zero, value).reshape(4, PB, 256)

    for part in range(4):
        proj_s[:, part * 256 : part * 256 + 256] = dot(
            normed, weight_in[which, :, pl.ds(part * 256, 256)]
        )
    for part in range(2):
        for half in range(2):
            at = pl.ds(half * 256, 256)
            value = proj_s[:, pl.ds(part * width + half * 256, 256)] * factor
            square = dot((value * value).astype(BF), same_head[...])
            value = value * lax.rsqrt(square + 1e-06)
            if part == 0:
                row = jnp.zeros((1, 256), F32)
                for n in range(4):
                    scale = scales[0, which, half * 4 + n] * (math.log2(math.e) / HEAD_DIM)
                    row = jnp.where(lane // HEAD_DIM == n, scale, row)
                q_s[:, at] = (value * row).astype(BF)
            else:
                put(ke_s, ko_s, at, value)
    for half in range(2):
        at = pl.ds(half * 256, 256)
        put(ve_s, vo_s, at, factor * dot(normed, weight_in[which, :, pl.ds(2 * width + half * 256, 256)]))


def twice_gelu(u):
    root = math.sqrt(2.0 / math.pi)
    return u + u * jnp.tanh(u * (root + (root * 0.044715) * (u * u)))


def time_stage(x, gains, scales, w_in, w_out, same_head, pair_sums, q_s, ke_s, ko_s, ve_s, vo_s, att_s, proj_s, weigh_s):
    normed, factor = rms(x, gains[0])
    project(normed, factor, 0, w_in, scales, same_head, q_s, ke_s, ko_s, ve_s, vo_s, proj_s)
    for a in range(2):
        rows = pl.ds(a * 128, 128)
        for j in range(4):
            at = pl.ds(j * 128, 128)
            keys = jnp.concatenate([k[2 * a + i, :, at] for k in (ke_s, ko_s) for i in range(2)], axis=0)
            weigh_s[:, pl.ds((a * 4 + j) * 256, 256)] = jnp.exp2(dot_nt(q_s[rows, at], keys)).astype(BF)
    for a in range(2):
        rows = pl.ds(a * 128, 128)
        for j in range(4):
            at = pl.ds(j * 128, 128)
            values = jnp.concatenate([v[2 * a + i, :, at] for v in (ve_s, vo_s) for i in range(2)], axis=0)
            mixed = dot(
                weigh_s[:, pl.ds((a * 4 + j) * 256, 256)],
                jnp.concatenate([values, pair_sums[...]], axis=1),
            )
            att_s[rows, at] = (mixed[:, :128] / mixed[:, 128:]).astype(BF)
    return (x.astype(F32) + dot(att_s[...], w_out[0])).astype(BF)


def patch_stage(
    x, vis, gains, scales, w_in, w_out, same_head, pair_sums, q_s, ke_s, ko_s, ve_s, vo_s, att_s, proj_s, weigh_s
):
    normed, factor = rms(x, gains[1])
    project(normed, factor, 1, w_in, scales, same_head, q_s, ke_s, ko_s, ve_s, vo_s, proj_s)
    even = iota((1, 128), 1) < HEAD_DIM
    even_pair = iota((1, 256), 1) % 128 < HEAD_DIM
    zero = jnp.zeros((PB, 128), BF)
    ones = jnp.ones((128, 128), BF)
    for b in range(4):
        rows = pl.ds(b * PB, PB)
        seen = [vis[i, b] for i in range(KV)]
        for j in range(4):
            at = pl.ds(j * 128, 128)
            keys = jnp.concatenate([ke_s[z, :, at] for z in seen], axis=0)
            queries = q_s[rows, at]
            queries = jnp.concatenate(
                [jnp.where(even, queries, zero), jnp.where(even, zero, queries)], axis=0
            )
            weigh_s[:, pl.ds((b * 4 + j) * 128, 128)] = jnp.exp2(dot_nt(queries, keys)).astype(BF)
    for b in range(4):
        rows = pl.ds(b * PB, PB)
        seen = [vis[i, b] for i in range(KV)]
        for j in range(4):
            at = pl.ds(j * 128, 128)
            values = jnp.concatenate([ve_s[z, :, at] for z in seen], axis=0)
            mixed = dot(
                weigh_s[:, pl.ds((b * 4 + j) * 128, 128)], jnp.concatenate([values, ones], axis=1)
            )
            mixed = jnp.where(even_pair, mixed[:PB], mixed[PB:])
            att_s[rows, at] = (mixed[:, :128] / mixed[:, 128:]).astype(BF)
    return (x.astype(F32) + dot(att_s[...], w_out[1])).astype(BF)


def feed_forward(x, gains, up, down, hidden, proj_s):
    normed, factor = rms(x, gains[2])
    for part in range(2):
        for c in range(4):
            at = pl.ds(c * 256, 256)
            proj_s[:, at] = dot(normed, up[:, pl.ds(part * 1024 + c * 256, 256)])
        for c in range(4):
            at = pl.ds(c * 256, 256)
            hidden[:, pl.ds(part * 1024 + c * 256, 256)] = twice_gelu(proj_s[:, at] * factor).astype(BF)
    return (x.astype(F32) + 0.5 * dot(hidden[...], down[...])).astype(BF)


def hour_order(h, n_hour, with_self):
    half = n_hour // 2
    steps = [half] + [k for i in range(half - 1, 0, -1) for k in (i, n_hour - i)] + [0] * with_self
    return [(k, lax.rem(h + k, n_hour)) for k in steps]


def patch_order(p, n_patch, with_self):
    x, y, c = p // 4, lax.rem(p // 2, 2), lax.rem(p, 2)
    steps = [(dx, dy, dc) for dy in (1, 0) for dx in (2, 1, 3, 0) for dc in (0, 1)]
    steps.sort(key=lambda t: (-(min(t[0], 4 - t[0]) + 2 * t[1]), -t[2]))
    order = []
    for k, (dx, dy, dc) in enumerate(steps):
        if (dx, dy, dc) != (0, 0, 0) or with_self:
            d = lax.rem(x + dx, n_patch // 4) * 4 + lax.rem(y + dy, 2) * 2 + lax.rem(c + dc, 2)
            order.append((k, d))
    return order


def all_order(p, h, n_patch, n_hour):
    patches = {}
    for t in [(dx, dy, dc) for dy in (1, 0) for dx in (2, 1, 3, 0) for dc in (0, 1)]:
        x, y, c = p // 4, lax.rem(p // 2, 2), lax.rem(p, 2)
        d = lax.rem(x + t[0], n_patch // 4) * 4 + lax.rem(y + t[1], 2) * 2 + lax.rem(c + t[2], 2)
        patches[t] = (min(t[0], 4 - t[0]) + 2 * t[1], d)
    hours = {k: (min(k, n_hour - k), d) for k, d in hour_order(h, n_hour, True)}
    pairs = [(hops + hop, d, e) for hops, d in patches.values() for hop, e in hours.values()]
    pairs.sort(key=lambda t: -t[0])
    return [(d, e) for hops, d, e in pairs if not (d is patches[(0, 0, 0)][1] and e is hours[0][1])]


def loop(start, stop, body):
    def step(i, carry):
        body(i)
        return carry

    lax.fori_loop(start, stop, step, 0)


def kernel(
    n_patch,
    n_hour,
    vis,
    scales,
    gains,
    inputs,
    w_in_hbm,
    w_out_hbm,
    up_hbm,
    down_hbm,
    out,
    w_in,
    w_out,
    up,
    down,
    timed,
    arrived,
    mixed,
    spread,
    handed,
    result,
    x_s,
    apart,
    weave,
    same_head,
    pair_sums,
    q_s,
    ke_s,
    ko_s,
    ve_s,
    vo_s,
    att_s,
    proj_s,
    weigh_s,
    hidden,
    w_sem,
    timed_sem,
    arrived_sem,
    spread_sem,
    back_sem,
    in_send,
    mixed_send,
    handed_send,
    result_send,
    final_send,
):
    s = lax.axis_index("pipe")
    p = lax.axis_index("patch")
    h = lax.axis_index("hour")

    loads = [
        pltpu.make_async_copy(src.at[0], dst, w_sem.at[i])
        for i, (src, dst) in enumerate(
            [(w_in_hbm, w_in), (w_out_hbm, w_out), (up_hbm, up), (down_hbm, down)]
        )
    ]
    for load in loads:
        load.start()

    def at16(i):
        return pl.ds(pl.multiple_of(i * 16, 16), 16)

    def remote(src, dst, send, recv, device):
        pltpu.make_async_remote_copy(
            src_ref=src,
            dst_ref=dst,
            send_sem=send,
            recv_sem=recv,
            device_id=device,
            device_id_type=MESH,
        ).start()

    def arrive(ref, sem):
        pltpu.make_async_copy(ref, ref, sem).wait()

    barrier = pltpu.get_barrier_semaphore()

    def greet(device):
        pl.semaphore_signal(barrier, inc=1, device_id=device, device_id_type=MESH)

    loop(1, n_hour, lambda k: greet((s, p, lax.rem(h + k, n_hour))))
    loop(1, n_patch, lambda k: greet((s, lax.rem(p + k, n_patch), h)))
    loop(0, n_hour, lambda k: greet((1 - s, p, k)))

    fill_constants(apart, weave, same_head, pair_sums)

    pl.semaphore_wait(barrier, (n_hour - 1) + (n_patch - 1) + n_hour)
    me = p * n_hour + h
    hour = h * n_patch + p

    for m in range(2):
        own = (inputs.at[m, 2 * h + s], timed.at[m, s, at16(h)])
        for k, d in hour_order(h, n_hour, False):
            remote(
                inputs.at[m, 2 * d + s], own[1], in_send.at[m, k], timed_sem.at[m, s, h], (0, p, d)
            )

        @pl.when(s == 0)
        def _(m=m, own=own):
            pltpu.make_async_copy(*own, timed_sem.at[m, 0, h]).start()

        @pl.when(s == 1)
        def _(m=m, own=own):
            remote(*own, in_send.at[m, 0], timed_sem.at[m, 1, h], (0, p, h))

    loads[0].wait()
    loads[1].wait()

    def time_step(m):
        @pl.when(s == 0)
        def _():
            for a in range(2):
                loop(0, n_hour, lambda k: arrive(timed.at[m, a, at16(k)], timed_sem.at[m, a, k]))

            x_s[...] = timed[m].reshape(256, 512)

        @pl.when(s == 1)
        def _():
            arrive(arrived.at[m], arrived_sem.at[m])
            x_s[...] = dot(apart[...], arrived[m].reshape(256, 512)).astype(BF)

        y = time_stage(
            x_s[...],
            gains,
            scales,
            w_in,
            w_out,
            same_head,
            pair_sums,
            q_s,
            ke_s,
            ko_s,
            ve_s,
            vo_s,
            att_s,
            proj_s,
            weigh_s,
        )
        mixed[m] = dot(weave[...], y).astype(BF).reshape(128, 2, 512)
        for d, e in all_order(p, h, n_patch, n_hour):
            remote(
                mixed.at[m, e * n_patch + d],
                spread.at[m, me],
                mixed_send.at[m],
                spread_sem.at[m],
                (s, d, e),
            )
        pltpu.make_async_copy(mixed.at[m, hour], spread.at[m, me], spread_sem.at[m]).start()

    loop(0, 2, time_step)
    loads[2].wait()
    loads[3].wait()

    def patch_step(m):
        arrive(spread.at[m], spread_sem.at[m])
        y = patch_stage(
            spread[m].reshape(256, 512),
            vis,
            gains,
            scales,
            w_in,
            w_out,
            same_head,
            pair_sums,
            q_s,
            ke_s,
            ko_s,
            ve_s,
            vo_s,
            att_s,
            proj_s,
            weigh_s,
        )
        x_s[...] = feed_forward(y, gains, up, down, hidden, proj_s)

        @pl.when(s == 0)
        def _():
            handed[m] = x_s[...].reshape(128, 2, 512)
            for d, e in all_order(p, h, n_patch, n_hour) + [(p, h)]:
                remote(
                    handed.at[m, d * n_hour + e],
                    arrived.at[m, hour],
                    handed_send.at[m],
                    arrived_sem.at[m],
                    (1, d, e),
                )

        @pl.when(s == 1)
        def _():
            result[m] = x_s[...]
            for k, d in patch_order(p, n_patch, True):
                for q in (0, 1):
                    if q == 0 or k < n_patch - 1:
                        remote(
                            result.at[m, at16(d)],
                            out.at[m, p],
                            (final_send, result_send)[q].at[m, k],
                            back_sem.at[m, p],
                            (q, d, h),
                        )
            pltpu.make_async_copy(result.at[m, at16(p)], out.at[m, p], back_sem.at[m, p]).start()

    loop(0, 2, patch_step)

    def finish(m):
        others = pl.ds(0, n_patch * n_hour - 1)
        arrive(mixed.at[m, others], mixed_send.at[m])
        loop(1, n_hour, lambda k: arrive(timed.at[0, 0, at16(k)], in_send.at[m, k]))

        @pl.when(s == 0)
        def _():
            arrive(handed.at[m], handed_send.at[m])

        @pl.when(s == 1)
        def _():
            arrive(timed.at[0, 0, at16(0)], in_send.at[m, 0])
            loop(0, n_patch, lambda k: arrive(result.at[m, at16(k)], final_send.at[m, k]))
            loop(0, n_patch - 1, lambda k: arrive(result.at[m, at16(k)], result_send.at[m, k]))

        loop(0, n_patch, lambda k: arrive(out.at[m, k], back_sem.at[m, k]))

    loop(0, 2, finish)


def solution(mesh):
    n_patch, n_hour = mesh.shape["patch"], mesh.shape["hour"]
    placed = (
        P(None, "patch", "hour", None),
        P(),
        P("pipe", None, None),
        P("pipe", None, None),
        P("pipe", None, None, None),
        P("pipe", None, None, None),
        P("pipe", None, None),
        P("pipe", None, None),
    )

    def local(inputs, visibility, norm_gains, scales, mixer_in, mixer_out, expand, reduce):
        tile = (256, 512)
        scratch = [
            pltpu.VMEM((2, 512, 1536), BF),
            pltpu.VMEM((2, 512, 512), BF),
            pltpu.VMEM((512, 2048), BF),
            pltpu.VMEM((2048, 512), BF),
            pltpu.VMEM((2, 2, 128, 512), BF),
            pltpu.VMEM((2, 128, 2, 512), BF),
            pltpu.VMEM((2, 128, 2, 512), BF),
            pltpu.VMEM((2, 128, 2, 512), BF),
            pltpu.VMEM((2, 128, 2, 512), BF),
            pltpu.VMEM((2, 256, 512), BF),
            pltpu.VMEM(tile, BF),
            pltpu.VMEM((256, 256), BF),
            pltpu.VMEM((256, 256), BF),
            pltpu.VMEM((256, 256), BF),
            pltpu.VMEM((256, 128), BF),
        ]
        scratch += [pltpu.VMEM(tile, BF)]
        scratch += [pltpu.VMEM((4, PB, 512), BF)] * 4
        scratch += [pltpu.VMEM(tile, BF)]
        scratch += [pltpu.VMEM((256, 1536), F32)]
        scratch += [pltpu.VMEM((128, 2048), BF)]
        scratch += [pltpu.VMEM((256, 2048), BF)]
        dma = pltpu.SemaphoreType.DMA
        scratch += [
            dma((4,)),
            dma((2, 2, n_hour)),
            dma((2,)),
            dma((2,)),
            dma((2, n_patch)),
            dma((2, n_hour)),
            dma((2,)),
            dma((2,)),
            dma((2, n_patch)),
            dma((2, n_patch)),
        ]
        smem = pl.BlockSpec(memory_space=pltpu.SMEM)
        hbm = pl.BlockSpec(memory_space=pl.ANY)
        by_hour = pl.pallas_call(
            functools.partial(kernel, n_patch, n_hour),
            out_shape=jax.ShapeDtypeStruct(inputs.shape, inputs.dtype),
            in_specs=[smem, smem, pl.BlockSpec(memory_space=pltpu.VMEM)] + [hbm] * 5,
            out_specs=hbm,
            scratch_shapes=scratch,
            compiler_params=pltpu.CompilerParams(collective_id=0, has_side_effects=True),
            name="space_time_blocks",
        )(
            visibility.T,
            scales,
            jnp.transpose(norm_gains, (1, 0, 2)),
            inputs,
            mixer_in,
            mixer_out,
            expand,
            reduce,
        )
        return jnp.swapaxes(by_hour, 1, 2)

    return jax.shard_map(
        local, mesh=mesh, in_specs=placed, out_specs=P(None, "patch", "hour", None), check_vma=False
    )
```

```python
import functools
import math

import jax
import jax.numpy as jnp
from jax import lax
from jax.experimental import pallas as pl
from jax.experimental.pallas import tpu as pltpu
from jax.sharding import PartitionSpec as P

HEADS = 8
HEAD_DIM = 64
PB = 64
KV = 2
BF = jnp.bfloat16
F32 = jnp.float32
MESH = pl.DeviceIdType.MESH


def iota(shape, axis):
    return lax.broadcasted_iota(jnp.int32, shape, axis)


def dot(a, b):
    return jnp.dot(a, b, preferred_element_type=F32)


def dot_nt(a, b):
    return lax.dot_general(a, b, (((1,), (1,)), ((), ())), preferred_element_type=F32)


def rms(x, gain):
    x = x.astype(F32)
    factor = lax.rsqrt(jnp.mean(x * x, axis=-1, keepdims=True) + 1e-05)
    return (x * gain).astype(BF), factor


def fill_constants(apart, weave, same_head, pair_sums):
    r, c = iota((256, 256), 0), iota((256, 256), 1)
    apart[...] = jnp.where(c == 2 * (r % 128) + r // 128, 1.0, 0.0).astype(BF)
    weave[...] = jnp.where(c == (r % 2) * 128 + r // 2, 1.0, 0.0).astype(BF)
    same_head[...] = jnp.where(r // HEAD_DIM == c // HEAD_DIM, 1.0 / HEAD_DIM, 0.0).astype(BF)
    r, c = iota((256, 128), 0), iota((256, 128), 1)
    pair_sums[...] = jnp.where(r // 128 == c // HEAD_DIM, 1.0, 0.0).astype(BF)


def project(normed, factor, which, weight_in, scales, same_head, q_s, ke_s, ko_s, ve_s, vo_s, proj_s):
    width = 2 * 256
    lane = iota((1, 256), 1)
    even = (lane // HEAD_DIM) % 2 == 0
    zero = jnp.zeros((256, 256), BF)

    def put(even_s, odd_s, at, value):
        value = value.astype(BF)
        if which == 1:
            even_s[:, :, at] = value.reshape(4, PB, 256)
        else:
            even_s[:, :, at] = jnp.where(even, value, zero).reshape(4, PB, 256)
            odd_s[:, :, at] = jnp.where(even, zero, value).reshape(4, PB, 256)

    for part in range(4):
        proj_s[:, part * 256 : part * 256 + 256] = dot(
            normed, weight_in[which, :, pl.ds(part * 256, 256)]
        )
    for part in range(2):
        for half in range(2):
            at = pl.ds(half * 256, 256)
            value = proj_s[:, pl.ds(part * width + half * 256, 256)] * factor
            square = dot((value * value).astype(BF), same_head[...])
            value = value * lax.rsqrt(square + 1e-06)
            if part == 0:
                row = jnp.zeros((1, 256), F32)
                for n in range(4):
                    scale = scales[0, which, half * 4 + n] * (math.log2(math.e) / HEAD_DIM)
                    row = jnp.where(lane // HEAD_DIM == n, scale, row)
                q_s[:, at] = (value * row).astype(BF)
            else:
                put(ke_s, ko_s, at, value)
    for half in range(2):
        at = pl.ds(half * 256, 256)
        put(ve_s, vo_s, at, factor * dot(normed, weight_in[which, :, pl.ds(2 * width + half * 256, 256)]))


def twice_gelu(u):
    root = math.sqrt(2.0 / math.pi)
    return u + u * jnp.tanh(u * (root + (root * 0.044715) * (u * u)))


def time_stage(x, gains, scales, w_in, w_out, same_head, pair_sums, q_s, ke_s, ko_s, ve_s, vo_s, att_s, proj_s, weigh_s):
    normed, factor = rms(x, gains[0])
    project(normed, factor, 0, w_in, scales, same_head, q_s, ke_s, ko_s, ve_s, vo_s, proj_s)
    for a in range(2):
        rows = pl.ds(a * 128, 128)
        for j in range(4):
            at = pl.ds(j * 128, 128)
            keys = jnp.concatenate([k[2 * a + i, :, at] for k in (ke_s, ko_s) for i in range(2)], axis=0)
            weigh_s[:, pl.ds((a * 4 + j) * 256, 256)] = jnp.exp2(dot_nt(q_s[rows, at], keys)).astype(BF)
    for a in range(2):
        rows = pl.ds(a * 128, 128)
        for j in range(4):
            at = pl.ds(j * 128, 128)
            values = jnp.concatenate([v[2 * a + i, :, at] for v in (ve_s, vo_s) for i in range(2)], axis=0)
            mixed = dot(
                weigh_s[:, pl.ds((a * 4 + j) * 256, 256)],
                jnp.concatenate([values, pair_sums[...]], axis=1),
            )
            att_s[rows, at] = (mixed[:, :128] / mixed[:, 128:]).astype(BF)
    return (x.astype(F32) + dot(att_s[...], w_out[0])).astype(BF)


def patch_stage(
    x, vis, gains, scales, w_in, w_out, same_head, pair_sums, q_s, ke_s, ko_s, ve_s, vo_s, att_s, proj_s, weigh_s
):
    normed, factor = rms(x, gains[1])
    project(normed, factor, 1, w_in, scales, same_head, q_s, ke_s, ko_s, ve_s, vo_s, proj_s)
    even = iota((1, 128), 1) < HEAD_DIM
    even_pair = iota((1, 256), 1) % 128 < HEAD_DIM
    zero = jnp.zeros((PB, 128), BF)
    ones = jnp.ones((128, 128), BF)
    for b in range(4):
        rows = pl.ds(b * PB, PB)
        seen = [vis[i, b] for i in range(KV)]
        for j in range(4):
            at = pl.ds(j * 128, 128)
            keys = jnp.concatenate([ke_s[z, :, at] for z in seen], axis=0)
            queries = q_s[rows, at]
            queries = jnp.concatenate(
                [jnp.where(even, queries, zero), jnp.where(even, zero, queries)], axis=0
            )
            weigh_s[:, pl.ds((b * 4 + j) * 128, 128)] = jnp.exp2(dot_nt(queries, keys)).astype(BF)
    for b in range(4):
        rows = pl.ds(b * PB, PB)
        seen = [vis[i, b] for i in range(KV)]
        for j in range(4):
            at = pl.ds(j * 128, 128)
            values = jnp.concatenate([ve_s[z, :, at] for z in seen], axis=0)
            mixed = dot(
                weigh_s[:, pl.ds((b * 4 + j) * 128, 128)], jnp.concatenate([values, ones], axis=1)
            )
            mixed = jnp.where(even_pair, mixed[:PB], mixed[PB:])
            att_s[rows, at] = (mixed[:, :128] / mixed[:, 128:]).astype(BF)
    return (x.astype(F32) + dot(att_s[...], w_out[1])).astype(BF)


def feed_forward(x, gains, up, down, hidden, proj_s):
    normed, factor = rms(x, gains[2])
    for part in range(2):
        for c in range(4):
            at = pl.ds(c * 256, 256)
            proj_s[:, at] = dot(normed, up[:, pl.ds(part * 1024 + c * 256, 256)])
        for c in range(4):
            at = pl.ds(c * 256, 256)
            hidden[:, pl.ds(part * 1024 + c * 256, 256)] = twice_gelu(proj_s[:, at] * factor).astype(BF)
    return (x.astype(F32) + 0.5 * dot(hidden[...], down[...])).astype(BF)


def hour_order(h, n_hour, with_self):
    half = n_hour // 2
    steps = [half] + [k for i in range(half - 1, 0, -1) for k in (i, n_hour - i)] + [0] * with_self
    return [(k, lax.rem(h + k, n_hour)) for k in steps]


def patch_order(p, n_patch, with_self):
    x, y, c = p // 4, lax.rem(p // 2, 2), lax.rem(p, 2)
    steps = [(dx, dy, dc) for dy in (1, 0) for dx in (2, 1, 3, 0) for dc in (0, 1)]
    steps.sort(key=lambda t: (-(min(t[0], 4 - t[0]) + 2 * t[1]), -t[2]))
    order = []
    for k, (dx, dy, dc) in enumerate(steps):
        if (dx, dy, dc) != (0, 0, 0) or with_self:
            d = lax.rem(x + dx, n_patch // 4) * 4 + lax.rem(y + dy, 2) * 2 + lax.rem(c + dc, 2)
            order.append((k, d))
    return order


def all_order(p, h, n_patch, n_hour):
    patches = {}
    for t in [(dx, dy, dc) for dy in (1, 0) for dx in (2, 1, 3, 0) for dc in (0, 1)]:
        x, y, c = p // 4, lax.rem(p // 2, 2), lax.rem(p, 2)
        d = lax.rem(x + t[0], n_patch // 4) * 4 + lax.rem(y + t[1], 2) * 2 + lax.rem(c + t[2], 2)
        patches[t] = (min(t[0], 4 - t[0]) + 2 * t[1], d)
    hours = {k: (min(k, n_hour - k), d) for k, d in hour_order(h, n_hour, True)}
    pairs = [(hops + hop, d, e) for hops, d in patches.values() for hop, e in hours.values()]
    pairs.sort(key=lambda t: -t[0])
    return [(d, e) for hops, d, e in pairs if not (d is patches[(0, 0, 0)][1] and e is hours[0][1])]


def loop(start, stop, body):
    def step(i, carry):
        body(i)
        return carry

    lax.fori_loop(start, stop, step, 0)


def kernel(
    n_patch,
    n_hour,
    vis,
    scales,
    gains,
    inputs,
    w_in_hbm,
    w_out_hbm,
    up_hbm,
    down_hbm,
    out,
    w_in,
    w_out,
    up,
    down,
    timed,
    arrived,
    mixed,
    spread,
    handed,
    result,
    x_s,
    apart,
    weave,
    same_head,
    pair_sums,
    q_s,
    ke_s,
    ko_s,
    ve_s,
    vo_s,
    att_s,
    proj_s,
    weigh_s,
    hidden,
    w_sem,
    timed_sem,
    arrived_sem,
    spread_sem,
    back_sem,
    in_send,
    mixed_send,
    handed_send,
    result_send,
    final_send,
):
    s = lax.axis_index("pipe")
    p = lax.axis_index("patch")
    h = lax.axis_index("hour")

    loads = [
        pltpu.make_async_copy(src.at[0], dst, w_sem.at[i])
        for i, (src, dst) in enumerate(
            [(w_in_hbm, w_in), (w_out_hbm, w_out), (up_hbm, up), (down_hbm, down)]
        )
    ]
    for load in loads:
        load.start()

    def at16(i):
        return pl.ds(pl.multiple_of(i * 16, 16), 16)

    def remote(src, dst, send, recv, device):
        pltpu.make_async_remote_copy(
            src_ref=src,
            dst_ref=dst,
            send_sem=send,
            recv_sem=recv,
            device_id=device,
            device_id_type=MESH,
        ).start()

    def arrive(ref, sem):
        pltpu.make_async_copy(ref, ref, sem).wait()

    barrier = pltpu.get_barrier_semaphore()

    def greet(device):
        pl.semaphore_signal(barrier, inc=1, device_id=device, device_id_type=MESH)

    for k, d in hour_order(h, n_hour, True):
        greet((1 - s, p, d))
    for k, d in hour_order(h, n_hour, False):
        greet((s, p, d))
    for k, d in patch_order(p, n_patch, False):
        greet((s, d, h))

    fill_constants(apart, weave, same_head, pair_sums)

    pl.semaphore_wait(barrier, (n_hour - 1) + (n_patch - 1) + n_hour)
    me = p * n_hour + h
    hour = h * n_patch + p

    for m in range(2):
        own = (inputs.at[m, 2 * h + s], timed.at[m, s, at16(h)])
        for k, d in hour_order(h, n_hour, False):
            remote(
                inputs.at[m, 2 * d + s], own[1], in_send.at[m, k], timed_sem.at[m, s, h], (0, p, d)
            )

        @pl.when(s == 0)
        def _(m=m, own=own):
            pltpu.make_async_copy(*own, timed_sem.at[m, 0, h]).start()

        @pl.when(s == 1)
        def _(m=m, own=own):
            remote(*own, in_send.at[m, 0], timed_sem.at[m, 1, h], (0, p, h))

    loads[0].wait()
    loads[1].wait()

    def time_step(m):
        @pl.when(s == 0)
        def _():
            for a in range(2):
                loop(0, n_hour, lambda k: arrive(timed.at[m, a, at16(k)], timed_sem.at[m, a, k]))

            x_s[...] = timed[m].reshape(256, 512)

        @pl.when(s == 1)
        def _():
            arrive(arrived.at[m], arrived_sem.at[m])
            x_s[...] = dot(apart[...], arrived[m].reshape(256, 512)).astype(BF)

        y = time_stage(
            x_s[...],
            gains,
            scales,
            w_in,
            w_out,
            same_head,
            pair_sums,
            q_s,
            ke_s,
            ko_s,
            ve_s,
            vo_s,
            att_s,
            proj_s,
            weigh_s,
        )
        mixed[m] = dot(weave[...], y).astype(BF).reshape(128, 2, 512)
        for d, e in all_order(p, h, n_patch, n_hour):
            remote(
                mixed.at[m, e * n_patch + d],
                spread.at[m, me],
                mixed_send.at[m],
                spread_sem.at[m],
                (s, d, e),
            )
        pltpu.make_async_copy(mixed.at[m, hour], spread.at[m, me], spread_sem.at[m]).start()

    loop(0, 2, time_step)
    loads[2].wait()
    loads[3].wait()

    def patch_step(m):
        arrive(spread.at[m], spread_sem.at[m])
        y = patch_stage(
            spread[m].reshape(256, 512),
            vis,
            gains,
            scales,
            w_in,
            w_out,
            same_head,
            pair_sums,
            q_s,
            ke_s,
            ko_s,
            ve_s,
            vo_s,
            att_s,
            proj_s,
            weigh_s,
        )
        x_s[...] = feed_forward(y, gains, up, down, hidden, proj_s)

        @pl.when(s == 0)
        def _():
            handed[m] = x_s[...].reshape(128, 2, 512)
            for d, e in all_order(p, h, n_patch, n_hour) + [(p, h)]:
                remote(
                    handed.at[m, d * n_hour + e],
                    arrived.at[m, hour],
                    handed_send.at[m],
                    arrived_sem.at[m],
                    (1, d, e),
                )

        @pl.when(s == 1)
        def _():
            result[m] = x_s[...]
            for k, d in patch_order(p, n_patch, True):
                for q in (0, 1):
                    if q == 0 or k < n_patch - 1:
                        remote(
                            result.at[m, at16(d)],
                            out.at[m, p],
                            (final_send, result_send)[q].at[m, k],
                            back_sem.at[m, p],
                            (q, d, h),
                        )
            pltpu.make_async_copy(result.at[m, at16(p)], out.at[m, p], back_sem.at[m, p]).start()

    loop(0, 2, patch_step)

    def finish(m):
        others = pl.ds(0, n_patch * n_hour - 1)
        arrive(mixed.at[m, others], mixed_send.at[m])
        loop(1, n_hour, lambda k: arrive(timed.at[0, 0, at16(k)], in_send.at[m, k]))

        @pl.when(s == 0)
        def _():
            arrive(handed.at[m], handed_send.at[m])

        @pl.when(s == 1)
        def _():
            arrive(timed.at[0, 0, at16(0)], in_send.at[m, 0])
            loop(0, n_patch, lambda k: arrive(result.at[m, at16(k)], final_send.at[m, k]))
            loop(0, n_patch - 1, lambda k: arrive(result.at[m, at16(k)], result_send.at[m, k]))

        loop(0, n_patch, lambda k: arrive(out.at[m, k], back_sem.at[m, k]))

    loop(0, 2, finish)


def solution(mesh):
    n_patch, n_hour = mesh.shape["patch"], mesh.shape["hour"]
    placed = (
        P(None, "patch", "hour", None),
        P(),
        P("pipe", None, None),
        P("pipe", None, None),
        P("pipe", None, None, None),
        P("pipe", None, None, None),
        P("pipe", None, None),
        P("pipe", None, None),
    )

    def local(inputs, visibility, norm_gains, scales, mixer_in, mixer_out, expand, reduce):
        tile = (256, 512)
        scratch = [
            pltpu.VMEM((2, 512, 1536), BF),
            pltpu.VMEM((2, 512, 512), BF),
            pltpu.VMEM((512, 2048), BF),
            pltpu.VMEM((2048, 512), BF),
            pltpu.VMEM((2, 2, 128, 512), BF),
            pltpu.VMEM((2, 128, 2, 512), BF),
            pltpu.VMEM((2, 128, 2, 512), BF),
            pltpu.VMEM((2, 128, 2, 512), BF),
            pltpu.VMEM((2, 128, 2, 512), BF),
            pltpu.VMEM((2, 256, 512), BF),
            pltpu.VMEM(tile, BF),
            pltpu.VMEM((256, 256), BF),
            pltpu.VMEM((256, 256), BF),
            pltpu.VMEM((256, 256), BF),
            pltpu.VMEM((256, 128), BF),
        ]
        scratch += [pltpu.VMEM(tile, BF)]
        scratch += [pltpu.VMEM((4, PB, 512), BF)] * 4
        scratch += [pltpu.VMEM(tile, BF)]
        scratch += [pltpu.VMEM((256, 1536), F32)]
        scratch += [pltpu.VMEM((128, 2048), BF)]
        scratch += [pltpu.VMEM((256, 2048), BF)]
        dma = pltpu.SemaphoreType.DMA
        scratch += [
            dma((4,)),
            dma((2, 2, n_hour)),
            dma((2,)),
            dma((2,)),
            dma((2, n_patch)),
            dma((2, n_hour)),
            dma((2,)),
            dma((2,)),
            dma((2, n_patch)),
            dma((2, n_patch)),
        ]
        smem = pl.BlockSpec(memory_space=pltpu.SMEM)
        hbm = pl.BlockSpec(memory_space=pl.ANY)
        by_hour = pl.pallas_call(
            functools.partial(kernel, n_patch, n_hour),
            out_shape=jax.ShapeDtypeStruct(inputs.shape, inputs.dtype),
            in_specs=[smem, smem, pl.BlockSpec(memory_space=pltpu.VMEM)] + [hbm] * 5,
            out_specs=hbm,
            scratch_shapes=scratch,
            compiler_params=pltpu.CompilerParams(
                collective_id=0, has_side_effects=True, vmem_limit_bytes=33554432
            ),
            name="space_time_blocks",
        )(
            pltpu.with_memory_space_constraint(visibility.T, pltpu.HBM),
            pltpu.with_memory_space_constraint(scales, pltpu.HBM),
            pltpu.with_memory_space_constraint(jnp.transpose(norm_gains, (1, 0, 2)), pltpu.HBM),
            pltpu.with_memory_space_constraint(inputs, pltpu.HBM),
            pltpu.with_memory_space_constraint(mixer_in, pltpu.HBM),
            pltpu.with_memory_space_constraint(mixer_out, pltpu.HBM),
            pltpu.with_memory_space_constraint(expand, pltpu.HBM),
            pltpu.with_memory_space_constraint(reduce, pltpu.HBM),
        )
        return jnp.swapaxes(by_hour, 1, 2)

    return jax.shard_map(
        local, mesh=mesh, in_specs=placed, out_specs=P(None, "patch", "hour", None), check_vma=False
    )
```
